32 devices in a mesh: dp: 8 (over y, x, core), ctx: 4 (over z).
Axes of the slice: x: 2, y: 2, z: 4, core: 2. Of those that a mesh axis runs over, the one named last changes fastest.
Arguments:
- queries: bfloat16 [8192, 2048], P(('dp', 'ctx')), parts along dimension 0, may hold values from -18 to 18
- key_vectors: bfloat16 [8192, 2048], P(('dp', 'ctx')), parts along dimension 0, may hold values from -18 to 18
- value_vectors: bfloat16 [8192, 2048], P(('dp', 'ctx')), parts along dimension 0, may hold values from -6 to 6
- norm_gain: float32 [2048], replicated, may hold values from 0.1 to 1.9
- window_gain: float32 [2048], replicated, may hold values from 0.1 to 1.9
Outputs:
- mixed: bfloat16 [8192, 2048], P(('dp', 'ctx')), parts along dimension 0
The draws below stay inside these ranges and needn't reach their ends.
There are 8 independent parts, one for each index of `dp`. The reference program is written for one: setup_inputs(seed, part) draws one part's arguments, and reference() takes and returns one part's arrays. A program takes and returns all parts, laid end to end along the dimension named above; an argument that names none is the same for every part. Nothing has to cross between parts.
All inputs are finite; a program needn't handle non-finite values.
Results may differ from the reference program's by a relative error of at most 0.0037.
Values may be sent and summed in bfloat16 or wider, within the bound.
A program may use at most 128 MiB of HBM per device.

```python
import math
import jax
import jax.numpy as jnp
from jax import lax

HEADS = 16
HEAD = 128
D = 2048
WINDOW = 1024
TOK_DEV = 256
SEQ = 1024


def draw_queries(key, part):
    drawn = jnp.clip(jax.random.normal(jax.random.fold_in(key, 1), (SEQ, D), jnp.float32), -6.0, 6.0)
    return drawn.astype(jnp.bfloat16)


def draw_key_vectors(key, part):
    drawn = jnp.clip(jax.random.normal(jax.random.fold_in(key, 3), (SEQ, D), jnp.float32), -6.0, 6.0)
    return drawn.astype(jnp.bfloat16)


def level_of(own_key, extent, cuts, least, top_value):
    def one(position, parts):
        draws = jax.random.uniform(jax.random.fold_in(jax.random.fold_in(own_key, 6), position), (parts,), jnp.float32, least / len(cuts), top_value / len(cuts))
        return jnp.repeat(jnp.exp(draws), extent[position] // parts).reshape((-1,) + (1,) * (len(extent) - position - 1))

    level = one(*cuts[0])
    for cut in cuts[1:]:
        level = level * one(*cut)
    return level


def noise(rng, dims, deviation, most, shards=(), kind=jnp.bfloat16):
    entries = jax.random.normal(rng, dims, jnp.float32) * deviation
    if len(shards) > 0:
        entries = level_of(rng, dims, shards, -0.22, 0.18) * entries
    return jnp.clip(entries, min=-most, max=most).astype(kind)


def setup_inputs(seed: int = 0, part: int = 0) -> dict:
    splits = jax.random.split(jax.random.key(seed), 6)
    own_keys = jax.random.split(jax.random.fold_in(splits[5], part), 6)
    queries = draw_queries(jax.random.fold_in(jax.random.fold_in(splits[5], part), 71), part)
    key_vectors = draw_key_vectors(jax.random.fold_in(jax.random.fold_in(splits[5], part), 71), part)
    value_vectors = noise(own_keys[2], (SEQ, D), 1.0, 6.0, ((0, 4),))
    norm_gain = jnp.clip(1.0 + 0.18 * jax.random.normal(splits[3], (D,), jnp.float32), 0.1, 1.9)
    window_gain = jnp.clip(1.0 + 0.18 * jax.random.normal(splits[4], (D,), jnp.float32), 0.1, 1.9)
    return dict(queries=queries, key_vectors=key_vectors, value_vectors=value_vectors, norm_gain=norm_gain, window_gain=window_gain)


def feature_map(values):
    upcast = values.astype(jnp.float32)
    return jnp.where(upcast > 0, upcast + 1.0, jnp.exp(jnp.minimum(upcast, 0.0))).astype(jnp.bfloat16)

def reference(queries, key_vectors, value_vectors, norm_gain, window_gain):
    length = queries.shape[0]
    query_heads = queries.reshape(length, HEADS, HEAD).transpose(1, 0, 2)
    key_heads = key_vectors.reshape(length, HEADS, HEAD).transpose(1, 0, 2)
    value_heads = value_vectors.reshape(length, HEADS, HEAD).transpose(1, 0, 2)
    positions = jnp.arange(length)
    inside = (positions[:, None] >= positions[None, :]) & (positions[:, None] - positions[None, :] < WINDOW)
    scale = 1.0 / math.sqrt(HEAD)

    def attend(operands):
        query_head, key_head, value_head = operands
        scores = jnp.dot(query_head, key_head.T, preferred_element_type=jnp.float32) * scale
        scores = jnp.where(inside, scores, -jnp.inf)
        peak = lax.optimization_barrier(jnp.max(scores, axis=-1, keepdims=True))
        expos = jnp.exp(scores - peak)
        weights = (expos / lax.optimization_barrier(jnp.sum(expos, axis=-1, keepdims=True))).astype(jnp.bfloat16)
        return jnp.dot(weights, value_head, preferred_element_type=jnp.float32)
    attended = lax.map(attend, (query_heads, key_heads, value_heads)).transpose(1, 0, 2)
    windowed = attended * lax.rsqrt(lax.optimization_barrier(jnp.mean(attended * attended, axis=-1, keepdims=True)) + 1e-05)
    windowed = windowed * window_gain.astype(jnp.float32).reshape(HEADS, HEAD)
    blocks = length // TOK_DEV
    phi_query = feature_map(queries).reshape(blocks, TOK_DEV, HEADS, HEAD).astype(jnp.float32)
    phi_key = feature_map(key_vectors).reshape(blocks, TOK_DEV, HEADS, HEAD).astype(jnp.float32)
    value_blocks = value_vectors.reshape(blocks, TOK_DEV, HEADS, HEAD).astype(jnp.float32)
    block_state = jnp.einsum('cthe,cthf->chef', phi_key, value_blocks)
    shifted = jnp.concatenate([jnp.zeros_like(block_state[:1]), block_state[:-1]], axis=0)
    carried = jnp.cumsum(shifted, axis=0).astype(jnp.bfloat16).astype(jnp.float32)
    from_state = jnp.einsum('cthe,chef->cthf', phi_query, carried)
    affinity = jnp.einsum('cthe,cshe->chts', phi_query, phi_key)
    inner = jnp.arange(TOK_DEV)
    causal = inner[:, None] >= inner[None, :]
    affinity = jnp.where(causal, affinity, 0.0).astype(jnp.bfloat16).astype(jnp.float32)
    local_part = jnp.einsum('chts,cshf->cthf', affinity, value_blocks)
    linear = (from_state + local_part).reshape(length, HEADS, HEAD)
    normed = linear * lax.rsqrt(lax.optimization_barrier(jnp.mean(linear * linear, axis=-1, keepdims=True)) + 1e-05)
    normed = normed * norm_gain.astype(jnp.float32).reshape(HEADS, HEAD)
    return (windowed + normed).reshape(length, HEADS * HEAD).astype(jnp.bfloat16)
```

```python
import functools
import math

import jax
import jax.numpy as jnp
from jax import lax
from jax.experimental import pallas as pl
from jax.experimental.pallas import tpu as pltpu
from jax.sharding import PartitionSpec as P

HEAD = 128
WINDOW = 1024
EPS = 1e-05


def passed_along(value, axis, steps):
    count = lax.axis_size(axis)
    leading, last = (max(0, -steps), min(count, count - steps))
    return lax.ppermute(value, axis, [(source, source + steps) for source in range(leading, last)])


def entering(array, axis, combine, identity):
    peers, position = (lax.axis_size(axis), lax.axis_index(axis))
    everything = lax.all_gather(array.astype(jnp.bfloat16), axis)
    start = jnp.broadcast_to(jnp.asarray(identity, array.dtype), array.shape)

    def lap(k, before):
        reached = k < position
        new = combine(before, everything[k].astype(array.dtype))
        return jnp.where(reached, new, before)

    return lax.fori_loop(0, peers, lap, start)


def feature_map(values):
    upcast = values.astype(jnp.float32)
    return jnp.where(upcast > 0, upcast + 1.0, jnp.exp(jnp.minimum(upcast, 0.0))).astype(
        jnp.bfloat16
    )


def add_states(earlier, later):
    return earlier + later


def shards(queries, key_vectors, value_vectors, norm_gain, window_gain):
    tok_rows, model_width = queries.shape
    head_count = model_width // HEAD
    ctx_index = lax.axis_index("ctx")
    reach_blocks = WINDOW // tok_rows
    own_pair = (key_vectors, value_vectors)
    received = []
    travelling = own_pair
    for distance in range(reach_blocks):
        travelling = passed_along((travelling[0], travelling[1]), "ctx", 1)
        received.append(travelling)
    ordered = received[::-1] + [own_pair]
    window_keys = jnp.concatenate([member[0] for member in ordered], axis=0)
    window_values = jnp.concatenate([member[1] for member in ordered], axis=0)
    span_rows = window_keys.shape[0]
    query_place = ctx_index * tok_rows + jnp.arange(tok_rows, dtype=jnp.int32)
    key_place = (ctx_index - reach_blocks) * tok_rows + jnp.arange(span_rows, dtype=jnp.int32)
    inside = (
        (key_place[None, :] <= query_place[:, None])
        & (query_place[:, None] - key_place[None, :] < WINDOW)
        & (key_place[None, :] >= 0)
    )
    group_size = 4
    groups = head_count // group_size
    scale = 1.0 / math.sqrt(HEAD)

    def split_groups(matrix):
        return jnp.moveaxis(matrix.reshape(matrix.shape[0], groups, group_size, HEAD), 1, 0)

    def attend(operands):
        query_group, key_group, value_group = operands
        scores = (
            jnp.einsum("tge,sge->gts", query_group, key_group, preferred_element_type=jnp.float32)
            * scale
        )
        scores = jnp.where(inside[None], scores, -jnp.inf)
        peak = jnp.max(scores, axis=-1, keepdims=True)
        expos = jnp.exp(scores - peak)
        weights = (expos / jnp.sum(expos, axis=-1, keepdims=True)).astype(jnp.bfloat16)
        return jnp.einsum("gts,sge->tge", weights, value_group, preferred_element_type=jnp.float32)

    attended = lax.map(
        attend, (split_groups(queries), split_groups(window_keys), split_groups(window_values))
    )
    attended = jnp.moveaxis(attended, 0, 1).reshape(tok_rows, head_count, HEAD)
    windowed = attended * lax.rsqrt(jnp.mean(attended * attended, axis=-1, keepdims=True) + EPS)
    windowed = windowed * window_gain.reshape(head_count, HEAD)
    phi_query = feature_map(queries).reshape(tok_rows, head_count, HEAD)
    phi_key = feature_map(key_vectors).reshape(tok_rows, head_count, HEAD)
    value_heads = value_vectors.reshape(tok_rows, head_count, HEAD)
    local_state = jnp.einsum(
        "the,thf->hef", phi_key, value_heads, preferred_element_type=jnp.float32
    )
    carried = entering(local_state, "ctx", add_states, jnp.zeros_like(local_state))
    from_state = jnp.einsum(
        "the,hef->thf", phi_query, carried.astype(jnp.bfloat16), preferred_element_type=jnp.float32
    )
    affinity = jnp.einsum("the,she->hts", phi_query, phi_key, preferred_element_type=jnp.float32)
    inner = jnp.arange(tok_rows, dtype=jnp.int32)
    causal = inner[:, None] >= inner[None, :]
    affinity = jnp.where(causal[None], affinity, 0.0).astype(jnp.bfloat16)
    local_part = jnp.einsum(
        "hts,shf->thf", affinity, value_heads, preferred_element_type=jnp.float32
    )
    linear = from_state + local_part
    normed = linear * lax.rsqrt(jnp.mean(linear * linear, axis=-1, keepdims=True) + EPS)
    normed = normed * norm_gain.reshape(head_count, HEAD)
    return (windowed + normed).reshape(tok_rows, model_width).astype(jnp.bfloat16)


QA, QB, KK, VV, OA, OB, ST, SN = range(8)
K2, V2, K3, V3, O2, O3 = range(6)
EXP_SCALE = math.log2(math.e) / math.sqrt(HEAD)
LOW = -1e30


def nt(a, b):
    return lax.dot_general(a, b, (((1,), (1,)), ((), ())), preferred_element_type=jnp.float32)


def tn(a, b):
    return lax.dot_general(a, b, (((0,), (0,)), ((), ())), preferred_element_type=jnp.float32)


def tt(a, b):
    return lax.dot_general(a, b, (((0,), (1,)), ((), ())), preferred_element_type=jnp.float32)


def classes(heads):
    return heads // 8, heads // 2


def hub_kernel(
    q_ref, k_ref, v_ref, gn_ref, gw_ref, out_ref,
    qa, qb, kr, vr, oa_s, ob_s, st_s, sn_s, oa_r, ob_r, st_r, sn_r,
    q_own, k_own, v_own, early_k, early_v, whole_in, whole_out,
    send, recv, send_w, recv_w, loaded,
):
    tok, width = q_ref.shape
    heads = width // HEAD
    early, whole = classes(heads)
    me = lax.axis_index("ctx")
    MESH = pl.DeviceIdType.MESH

    def cols(h):
        if isinstance(h, int):
            return pl.ds(h * HEAD, HEAD)
        return pl.ds(pl.multiple_of(h * HEAD, HEAD), HEAD)

    def move(stream, src, dst, h, target):
        return pltpu.make_async_remote_copy(
            src_ref=src,
            dst_ref=dst,
            send_sem=send.at[stream, h],
            recv_sem=recv.at[stream, h],
            device_id={"ctx": target},
            device_id_type=MESH,
        )

    def move_whole(stream, src, dst, target):
        return pltpu.make_async_remote_copy(
            src_ref=src,
            dst_ref=dst,
            send_sem=send_w.at[stream],
            recv_sem=recv_w.at[stream],
            device_id={"ctx": target},
            device_id_type=MESH,
        )

    def q2_left(h):
        return move(QA, q_ref.at[:, cols(h)], qa.at[:, cols(h)], h, 1)

    def q3_left(h):
        return move(QA, q_ref.at[:, cols(h)], qa.at[:, cols(h)], h, 2)

    def q3_relay(h):
        return move(QB, qa.at[:, cols(h)], qb.at[:, cols(h)], h, 1)

    def k0_right(h):
        return move(KK, k_ref.at[:, cols(h)], kr.at[:, cols(h)], h, 1)

    def v0_right(h):
        return move(VV, v_ref.at[:, cols(h)], vr.at[:, cols(h)], h, 1)

    def k1_early(h):
        return move(KK, k_ref.at[:, cols(h)], early_k.at[1, h], h, 2)

    def v1_early(h):
        return move(VV, v_ref.at[:, cols(h)], early_v.at[1, h], h, 2)

    def k0_early(h):
        return move(KK, kr.at[:, cols(h)], early_k.at[0, h], early + h, 2)

    def v0_early(h):
        return move(VV, vr.at[:, cols(h)], early_v.at[0, h], early + h, 2)

    def k2_whole():
        return move_whole(K2, k_ref.at[:, cols(whole)], whole_in.at[0], 1)

    def v2_whole():
        return move_whole(V2, v_ref.at[:, cols(whole)], whole_in.at[1], 1)

    def k3_whole():
        return move_whole(K3, k_ref.at[:, cols(whole)], whole_in.at[2], 1)

    def v3_whole():
        return move_whole(V3, v_ref.at[:, cols(whole)], whole_in.at[3], 1)

    def q3_whole():
        return move(QB, q_ref.at[:, cols(whole)], qb.at[:, cols(whole)], whole, 1)

    def out2_whole():
        return move_whole(O2, whole_out.at[0], out_ref.at[:, cols(whole)], 2)

    def out3_whole():
        return move_whole(O3, whole_out.at[1], whole_out.at[2], 2)

    def out3_relay():
        return move_whole(O3, whole_out.at[2], out_ref.at[:, cols(whole)], 3)

    def oa_right(h, target):
        return move(OA, oa_s.at[h], oa_r.at[h], h, target)

    def ob_right(h):
        return move(OB, ob_s.at[h], ob_r.at[h], h, 2)

    def st_right(h, target):
        return move(ST, st_s.at[h], st_r.at[h], h, target)

    def sn_right(h, target):
        return move(SN, sn_s.at[h], sn_r.at[h], h, target)

    def each(start, stop, body):
        def step(h, carry):
            body(h)
            return carry

        lax.fori_loop(start, stop, step, 0)

    def split_heads(body):
        each(early, whole, body)
        each(whole + 1, heads, body)

    loads = [
        pltpu.make_async_copy(src, dst, loaded.at[i])
        for i, (src, dst) in enumerate([(k_ref, k_own), (v_ref, v_own), (q_ref, q_own)])
    ]
    for load in loads:
        load.start()

    barrier = pltpu.get_barrier_semaphore()
    senders = {1: (0, 2, 3), 2: (1, 3), 3: (2,)}
    for device, others in senders.items():

        @pl.when(me == device)
        def _():
            for other in others:
                pl.semaphore_signal(
                    barrier, inc=1, device_id={"ctx": other}, device_id_type=MESH
                )

    pl.semaphore_wait(barrier, 1 + (me >= 2).astype(jnp.int32))

    key_at = lax.broadcasted_iota(jnp.int32, (tok, tok), 0)
    query_at = lax.broadcasted_iota(jnp.int32, (tok, tok), 1)
    causal = key_at <= query_at

    def soft(scores, values):
        peak = functools.reduce(
            jnp.maximum, [jnp.max(s, axis=0, keepdims=True) for s in scores]
        )
        total, out = 0.0, 0.0
        for s, v in zip(scores, values):
            e = jnp.exp2((s - peak) * EXP_SCALE)
            total = total + jnp.sum(e, axis=0, keepdims=True)
            out = out + tn(v, e.astype(jnp.bfloat16))
        return peak, total, out

    def normalised(soft_sum):
        peak, total, out = soft_sum
        return peak + jnp.log2(total) * (1.0 / EXP_SCALE), out * (1.0 / total)

    def merge(one, level, out):
        top = jnp.maximum(one[0], level)
        f1 = jnp.exp2((one[0] - top) * EXP_SCALE)
        f2 = jnp.exp2((level - top) * EXP_SCALE)
        return top, one[1] * f1 + f2, one[2] * f1 + out.astype(jnp.float32) * f2

    def local_linear(q, phi_k, v):
        phi_q = feature_map(q)
        affinity = jnp.where(causal, nt(phi_k, phi_q), 0.0).astype(jnp.bfloat16)
        return phi_q, tn(v, affinity)

    def rows_of(h, soft_sum, linear):
        _, total, out = soft_sum
        att = out * (1.0 / total)
        att = att * lax.rsqrt(jnp.mean(att * att, axis=0, keepdims=True) + EPS)
        lin = linear * lax.rsqrt(jnp.mean(linear * linear, axis=0, keepdims=True) + EPS)
        row = att.T * gw_ref[pl.ds(h, 1), :] + lin.T * gn_ref[pl.ds(h, 1), :]
        return row.astype(jnp.bfloat16)

    def finish(h, soft_sum, linear):
        out_ref[:, cols(h)] = rows_of(h, soft_sum, linear)

    def diagonal(q, k):
        return jnp.where(causal, nt(k, q), LOW)

    @pl.when(me == 0)
    def _():
        def start(h):
            k0_right(h).start()
            v0_right(h).start()

        each(0, heads, start)

        for load in loads:
            load.wait()

        def compute(h):
            q, k, v = q_own[:, cols(h)], k_own[:, cols(h)], v_own[:, cols(h)]
            _, linear = local_linear(q, feature_map(k), v)
            finish(h, soft([diagonal(q, k)], [v]), linear)

        each(0, heads, compute)

        def drain(h):
            k0_right(h).wait_send()
            v0_right(h).wait_send()

        each(0, heads, drain)

    @pl.when(me == 1)
    def _():
        def start(h):
            k1_early(h).start()
            v1_early(h).start()

        each(0, early, start)

        for load in loads:
            load.wait()

        def own_rows(h, q, k, v, k0, v0, phi_k, before):
            phi_q, linear = local_linear(q, phi_k, v)
            linear = linear + tt(before.astype(jnp.bfloat16), phi_q)
            finish(h, soft([nt(k0, q), diagonal(q, k)], [v0, v]), linear)

        def early_head(h):
            q, k, v = q_own[:, cols(h)], k_own[:, cols(h)], v_own[:, cols(h)]
            k0_right(h).wait_recv()
            k0_early(h).start()
            v0_right(h).wait_recv()
            v0_early(h).start()
            k0, v0 = kr[:, cols(h)], vr[:, cols(h)]
            before = tn(feature_map(k0), v0)
            own_rows(h, q, k, v, k0, v0, feature_map(k), before)

        each(0, early, early_head)

        def shared_head(h):
            q, k, v = q_own[:, cols(h)], k_own[:, cols(h)], v_own[:, cols(h)]
            phi_k = feature_map(k)
            state = tn(phi_k, v)
            k0_right(h).wait_recv()
            v0_right(h).wait_recv()
            k0, v0 = kr[:, cols(h)], vr[:, cols(h)]
            before = tn(feature_map(k0), v0)
            sn_s[h] = (before + state).astype(jnp.bfloat16)
            sn_right(h, 2).start()

            def part(queries, row, target):
                other = queries[:, cols(h)]
                level, out = normalised(soft([nt(k0, other), nt(k, other)], [v0, v]))
                target[h] = out.astype(jnp.bfloat16)
                st_s[h, row : row + 1] = level

            q3_relay(h).wait_recv()
            part(qb, 1, ob_s)
            ob_right(h).start()
            q2_left(h).wait_recv()
            part(qa, 0, oa_s)
            st_right(h, 2).start()

            @pl.when(h < whole)
            def _():
                oa_right(h, 2).start()

            @pl.when(h > whole + 1)
            def _():
                oa_right(h - 1, 2).start()

            own_rows(h, q, k, v, k0, v0, phi_k, before)

        def whole_head(h):
            q, k, v = q_own[:, cols(h)], k_own[:, cols(h)], v_own[:, cols(h)]
            phi_k = feature_map(k)
            k0_right(h).wait_recv()
            v0_right(h).wait_recv()
            k0, v0 = kr[:, cols(h)], vr[:, cols(h)]
            before = tn(feature_map(k0), v0)
            own_rows(h, q, k, v, k0, v0, phi_k, before)
            before = before + tn(phi_k, v)
            q2_left(h).wait_recv()
            k2_whole().wait_recv()
            v2_whole().wait_recv()
            q2, k2, v2 = qa[:, cols(h)], whole_in[0], whole_in[1]
            phi_k2 = feature_map(k2)
            phi_q, linear = local_linear(q2, phi_k2, v2)
            linear = linear + tt(before.astype(jnp.bfloat16), phi_q)
            scores = [nt(k0, q2), nt(k, q2), diagonal(q2, k2)]
            whole_out[0] = rows_of(h, soft(scores, [v0, v, v2]), linear)
            before = before + tn(phi_k2, v2)
            q3_whole().wait_recv()
            k3_whole().wait_recv()
            v3_whole().wait_recv()
            q3, k3, v3 = qb[:, cols(h)], whole_in[2], whole_in[3]
            phi_q, linear = local_linear(q3, feature_map(k3), v3)
            linear = linear + tt(before.astype(jnp.bfloat16), phi_q)
            scores = [nt(k0, q3), nt(k, q3), nt(k2, q3), diagonal(q3, k3)]
            whole_out[1] = rows_of(h, soft(scores, [v0, v, v2, v3]), linear)
            out3_whole().start()

        def head(h):
            @pl.when(h == whole)
            def _():
                whole_head(whole)

            @pl.when(h != whole)
            def _():
                shared_head(h)

        each(early, heads, head)
        oa_right(heads - 1, 2).start()
        out2_whole().start()

        def drain_early(h):
            k1_early(h).wait_send()
            v1_early(h).wait_send()
            k0_early(h).wait_send()
            v0_early(h).wait_send()

        each(0, early, drain_early)

        def drain(h):
            sn_right(h, 2).wait_send()
            ob_right(h).wait_send()
            st_right(h, 2).wait_send()
            oa_right(h, 2).wait_send()

        split_heads(drain)
        out3_whole().wait_send()
        out2_whole().wait_send()

    @pl.when(me == 2)
    def _():
        def relay(h):
            @pl.when(h == whole)
            def _():
                q2_left(whole).start()
                k2_whole().start()
                v2_whole().start()

            @pl.when(h != whole)
            def _():
                q2_left(h).start()
                q3_left(h).wait_recv()
                q3_relay(h).start()

        each(early, heads, relay)

        for load in loads:
            load.wait()

        def pass_on(h, level, out):
            oa_s[h] = out.astype(jnp.bfloat16)
            st_s[h, 0:1] = level
            st_s[h, 1:2] = level
            st_right(h, 3).start()
            oa_right(h, 3).start()

        def early_head(h):
            q, k, v = q_own[:, cols(h)], k_own[:, cols(h)], v_own[:, cols(h)]
            k1_early(h).wait_recv()
            v1_early(h).wait_recv()
            k0_early(h).wait_recv()
            v0_early(h).wait_recv()
            q3_left(h).wait_recv()
            k0, v0, k1, v1 = early_k[0, h], early_v[0, h], early_k[1, h], early_v[1, h]
            phi_k = feature_map(k)
            before = tn(feature_map(k0), v0) + tn(feature_map(k1), v1)
            sn_s[h] = (before + tn(phi_k, v)).astype(jnp.bfloat16)
            sn_right(h, 3).start()
            q3 = qa[:, cols(h)]
            other = soft([nt(k0, q3), nt(k1, q3), nt(k, q3)], [v0, v1, v])
            pass_on(h, *normalised(other))
            phi_q, linear = local_linear(q, phi_k, v)
            linear = linear + tt(before.astype(jnp.bfloat16), phi_q)
            scores = [nt(k0, q), nt(k1, q), diagonal(q, k)]
            finish(h, soft(scores, [v0, v1, v]), linear)

        each(0, early, early_head)

        def for_last(h):
            k, v = k_own[:, cols(h)], v_own[:, cols(h)]
            state = tn(feature_map(k), v)
            other = soft([nt(k, qa[:, cols(h)])], [v])
            sn_right(h, 2).wait_recv()
            sn_s[h] = (sn_r[h].astype(jnp.float32) + state).astype(jnp.bfloat16)
            sn_right(h, 3).start()
            ob_right(h).wait_recv()
            st_right(h, 2).wait_recv()
            pass_on(h, *normalised(merge(other, st_r[h, 1:2], ob_r[h])))

        def for_own(h):
            q, k, v = q_own[:, cols(h)], k_own[:, cols(h)], v_own[:, cols(h)]
            phi_q, linear = local_linear(q, feature_map(k), v)
            linear = linear + tt(sn_r[h], phi_q)
            own = soft([diagonal(q, k)], [v])
            oa_right(h, 2).wait_recv()
            finish(h, merge(own, st_r[h, 0:1], oa_r[h]), linear)

        def head(h):
            @pl.when(h == whole)
            def _():
                out3_whole().wait_recv()
                out3_relay().start()

            @pl.when(h != whole)
            def _():
                for_last(h)

            late = (h > whole).astype(jnp.int32)

            @pl.when((h != whole) & (h != whole + 1))
            def _():
                for_own(h - late)

        each(early, heads, head)
        for_own(heads - 1)
        out2_whole().wait_recv()

        def drain_relay(h):
            q2_left(h).wait_send()
            q3_relay(h).wait_send()

        split_heads(drain_relay)
        q2_left(whole).wait_send()
        k2_whole().wait_send()
        v2_whole().wait_send()
        out3_relay().wait_send()

        def drain(h):
            st_right(h, 3).wait_send()
            oa_right(h, 3).wait_send()
            sn_right(h, 3).wait_send()

        each(0, whole, drain)
        each(whole + 1, heads, drain)

    @pl.when(me == 3)
    def _():
        def start(h):
            @pl.when(h == whole)
            def _():
                q3_whole().start()
                k3_whole().start()
                v3_whole().start()

            @pl.when(h != whole)
            def _():
                q3_left(h).start()

        each(early, heads, start)
        each(0, early, start)

        for load in loads:
            load.wait()

        def compute(h):
            q, k, v = q_own[:, cols(h)], k_own[:, cols(h)], v_own[:, cols(h)]
            phi_q, linear = local_linear(q, feature_map(k), v)
            own = soft([diagonal(q, k)], [v])
            sn_right(h, 3).wait_recv()
            linear = linear + tt(sn_r[h], phi_q)
            st_right(h, 3).wait_recv()
            oa_right(h, 3).wait_recv()
            finish(h, merge(own, st_r[h, 0:1], oa_r[h]), linear)

        each(0, whole, compute)
        out3_relay().wait_recv()
        each(whole + 1, heads, compute)

        def drain(h):
            q3_left(h).wait_send()

        each(0, whole, drain)
        each(whole + 1, heads, drain)
        q3_whole().wait_send()
        k3_whole().wait_send()
        v3_whole().wait_send()


def hub_shards(queries, key_vectors, value_vectors, norm_gain, window_gain):
    tok, width = queries.shape
    heads = width // HEAD
    early, _ = classes(heads)
    vmem = pl.BlockSpec(memory_space=pltpu.VMEM)
    hbm = pl.BlockSpec(memory_space=pl.ANY)
    block = pltpu.VMEM((tok, width), jnp.bfloat16)
    partial = pltpu.VMEM((heads, HEAD, tok), jnp.bfloat16)
    stats = pltpu.VMEM((heads, 2, tok), jnp.float32)
    state = pltpu.VMEM((heads, HEAD, HEAD), jnp.bfloat16)
    dma = pltpu.SemaphoreType.DMA
    return pl.pallas_call(
        hub_kernel,
        out_shape=pltpu.VMEM((tok, width), jnp.bfloat16),
        in_specs=[hbm] * 3 + [vmem] * 2,
        out_specs=vmem,
        scratch_shapes=[block] * 4
        + [partial, partial, stats, state] * 2
        + [block] * 3
        + [pltpu.VMEM((2, early, tok, HEAD), jnp.bfloat16)] * 2
        + [pltpu.VMEM((4, tok, HEAD), jnp.bfloat16), pltpu.VMEM((3, tok, HEAD), jnp.bfloat16)]
        + [dma((8, heads)), dma((8, heads)), dma((6,)), dma((6,)), dma((3,))],
        compiler_params=pltpu.CompilerParams(
            collective_id=0, has_side_effects=True, vmem_limit_bytes=56 * 2**20
        ),
        name="hub_attention",
    )(
        queries,
        key_vectors,
        value_vectors,
        norm_gain.reshape(heads, HEAD),
        window_gain.reshape(heads, HEAD),
    )


def solution(mesh):
    count = mesh.shape["ctx"]

    def run(queries, key_vectors, value_vectors, norm_gain, window_gain):
        args = (queries, key_vectors, value_vectors, norm_gain, window_gain)
        fits = count * queries.shape[0] <= WINDOW
        if fits and count == 4 and queries.shape[1] >= 8 * HEAD:
            return hub_shards(*args)
        return shards(*args)

    return jax.shard_map(
        run,
        mesh=mesh,
        in_specs=(P(("dp", "ctx"), None), P(("dp", "ctx"), None), P(("dp", "ctx"), None), P(), P()),
        out_specs=P(("dp", "ctx"), None),
        check_vma=False,
    )
```

```python
import functools
import math

import jax
import jax.numpy as jnp
from jax import lax
from jax.experimental import pallas as pl
from jax.experimental.pallas import tpu as pltpu
from jax.sharding import PartitionSpec as P

HEAD = 128
WINDOW = 1024
EPS = 1e-05


def passed_along(value, axis, steps):
    count = lax.axis_size(axis)
    leading, last = (max(0, -steps), min(count, count - steps))
    return lax.ppermute(value, axis, [(source, source + steps) for source in range(leading, last)])


def entering(array, axis, combine, identity):
    peers, position = (lax.axis_size(axis), lax.axis_index(axis))
    everything = lax.all_gather(array.astype(jnp.bfloat16), axis)
    start = jnp.broadcast_to(jnp.asarray(identity, array.dtype), array.shape)

    def lap(k, before):
        reached = k < position
        new = combine(before, everything[k].astype(array.dtype))
        return jnp.where(reached, new, before)

    return lax.fori_loop(0, peers, lap, start)


def feature_map(values):
    upcast = values.astype(jnp.float32)
    return jnp.where(upcast > 0, upcast + 1.0, jnp.exp(jnp.minimum(upcast, 0.0))).astype(
        jnp.bfloat16
    )


def add_states(earlier, later):
    return earlier + later


def shards(queries, key_vectors, value_vectors, norm_gain, window_gain):
    tok_rows, model_width = queries.shape
    head_count = model_width // HEAD
    ctx_index = lax.axis_index("ctx")
    reach_blocks = WINDOW // tok_rows
    own_pair = (key_vectors, value_vectors)
    received = []
    travelling = own_pair
    for distance in range(reach_blocks):
        travelling = passed_along((travelling[0], travelling[1]), "ctx", 1)
        received.append(travelling)
    ordered = received[::-1] + [own_pair]
    window_keys = jnp.concatenate([member[0] for member in ordered], axis=0)
    window_values = jnp.concatenate([member[1] for member in ordered], axis=0)
    span_rows = window_keys.shape[0]
    query_place = ctx_index * tok_rows + jnp.arange(tok_rows, dtype=jnp.int32)
    key_place = (ctx_index - reach_blocks) * tok_rows + jnp.arange(span_rows, dtype=jnp.int32)
    inside = (
        (key_place[None, :] <= query_place[:, None])
        & (query_place[:, None] - key_place[None, :] < WINDOW)
        & (key_place[None, :] >= 0)
    )
    group_size = 4
    groups = head_count // group_size
    scale = 1.0 / math.sqrt(HEAD)

    def split_groups(matrix):
        return jnp.moveaxis(matrix.reshape(matrix.shape[0], groups, group_size, HEAD), 1, 0)

    def attend(operands):
        query_group, key_group, value_group = operands
        scores = (
            jnp.einsum("tge,sge->gts", query_group, key_group, preferred_element_type=jnp.float32)
            * scale
        )
        scores = jnp.where(inside[None], scores, -jnp.inf)
        peak = jnp.max(scores, axis=-1, keepdims=True)
        expos = jnp.exp(scores - peak)
        weights = (expos / jnp.sum(expos, axis=-1, keepdims=True)).astype(jnp.bfloat16)
        return jnp.einsum("gts,sge->tge", weights, value_group, preferred_element_type=jnp.float32)

    attended = lax.map(
        attend, (split_groups(queries), split_groups(window_keys), split_groups(window_values))
    )
    attended = jnp.moveaxis(attended, 0, 1).reshape(tok_rows, head_count, HEAD)
    windowed = attended * lax.rsqrt(jnp.mean(attended * attended, axis=-1, keepdims=True) + EPS)
    windowed = windowed * window_gain.reshape(head_count, HEAD)
    phi_query = feature_map(queries).reshape(tok_rows, head_count, HEAD)
    phi_key = feature_map(key_vectors).reshape(tok_rows, head_count, HEAD)
    value_heads = value_vectors.reshape(tok_rows, head_count, HEAD)
    local_state = jnp.einsum(
        "the,thf->hef", phi_key, value_heads, preferred_element_type=jnp.float32
    )
    carried = entering(local_state, "ctx", add_states, jnp.zeros_like(local_state))
    from_state = jnp.einsum(
        "the,hef->thf", phi_query, carried.astype(jnp.bfloat16), preferred_element_type=jnp.float32
    )
    affinity = jnp.einsum("the,she->hts", phi_query, phi_key, preferred_element_type=jnp.float32)
    inner = jnp.arange(tok_rows, dtype=jnp.int32)
    causal = inner[:, None] >= inner[None, :]
    affinity = jnp.where(causal[None], affinity, 0.0).astype(jnp.bfloat16)
    local_part = jnp.einsum(
        "hts,shf->thf", affinity, value_heads, preferred_element_type=jnp.float32
    )
    linear = from_state + local_part
    normed = linear * lax.rsqrt(jnp.mean(linear * linear, axis=-1, keepdims=True) + EPS)
    normed = normed * norm_gain.reshape(head_count, HEAD)
    return (windowed + normed).reshape(tok_rows, model_width).astype(jnp.bfloat16)


EXP_SCALE = math.log2(math.e) / math.sqrt(HEAD)
LOW = -1e30


def nt(a, b):
    return lax.dot_general(a, b, (((1,), (1,)), ((), ())), preferred_element_type=jnp.float32)


def tn(a, b):
    return lax.dot_general(a, b, (((0,), (0,)), ((), ())), preferred_element_type=jnp.float32)


def tt(a, b):
    return lax.dot_general(a, b, (((0,), (1,)), ((), ())), preferred_element_type=jnp.float32)


def classes(heads):
    return heads // 8, heads // 2, heads - 1


def hub_kernel(
    q_ref, k_ref, v_ref, gn_ref, gw_ref, out_ref,
    kv0, qq, own, gains, early_kv, whole_in, whole_out, pack_s, pack_r, oa_s, oa_r, st_s, st_r,
    sem_a, sem_b, sem_c, sem_d, sem_w, sem_s, loaded,
):
    tok, width = q_ref.shape
    heads = width // HEAD
    early, cut, whole = classes(heads)
    depth = HEAD * HEAD // tok
    me = lax.axis_index("ctx")
    MESH = pl.DeviceIdType.MESH

    def cols(h):
        if isinstance(h, int):
            return pl.ds(h * HEAD, HEAD)
        return pl.ds(pl.multiple_of(h * HEAD, HEAD), HEAD)

    def move(src, dst, sent, arrived, target):
        return pltpu.make_async_remote_copy(
            src_ref=src,
            dst_ref=dst,
            send_sem=sent,
            recv_sem=arrived,
            device_id={"ctx": target},
            device_id_type=MESH,
        )

    def arrived(ref, sem):
        move(ref, ref, sem_s.at[0], sem, 0).wait_recv()

    def sent(ref, i):
        move(ref, ref, sem_s.at[i], sem_w.at[0], 0).wait_send()

    def each(start, stop, body):
        def step(h, carry):
            body(h)
            return carry

        lax.fori_loop(start, stop, step, 0)

    def in_turn(h, body):
        later = [(h >= at).astype(jnp.int32) for at in (cut, cut + 2)]

        @pl.when((h != cut) & (h != cut + 2))
        def _():
            body(h - later[0] - later[1])

    loads = [
        pltpu.make_async_copy(src, own.at[i], loaded.at[0])
        for i, src in enumerate([q_ref, k_ref, v_ref])
    ] + [
        pltpu.make_async_copy(src, gains.at[i], loaded.at[1])
        for i, src in enumerate([gn_ref, gw_ref])
    ]
    for load in loads:
        load.start()

    def wait_loads():
        pltpu.make_async_copy(own, own, loaded.at[0]).wait()
        pltpu.make_async_copy(gains, gains, loaded.at[1]).wait()

    barrier = pltpu.get_barrier_semaphore()
    senders = {1: (0, 2, 3), 2: (1, 3), 3: (2,)}
    for device, others in senders.items():

        @pl.when(me == device)
        def _():
            for other in others:
                pl.semaphore_signal(
                    barrier, inc=1, device_id={"ctx": other}, device_id_type=MESH
                )

    pl.semaphore_wait(barrier, 1 + (me >= 2).astype(jnp.int32))

    key_at = lax.broadcasted_iota(jnp.int32, (tok, tok), 0)
    query_at = lax.broadcasted_iota(jnp.int32, (tok, tok), 1)
    causal = key_at <= query_at

    def own_qkv(h):
        return own[0, :, cols(h)], own[1, :, cols(h)], own[2, :, cols(h)]

    def soft(scores, values):
        peak = functools.reduce(
            jnp.maximum, [jnp.max(s, axis=0, keepdims=True) for s in scores]
        )
        total, out = 0.0, 0.0
        for s, v in zip(scores, values):
            e = jnp.exp2((s - peak) * EXP_SCALE)
            total = total + jnp.sum(e, axis=0, keepdims=True)
            out = out + tn(v, e.astype(jnp.bfloat16))
        return peak, total, out

    def normalised(soft_sum):
        peak, total, out = soft_sum
        return peak + jnp.log2(total) * (1.0 / EXP_SCALE), out * (1.0 / total)

    def merge(one, level, out):
        top = jnp.maximum(one[0], level)
        f1 = jnp.exp2((one[0] - top) * EXP_SCALE)
        f2 = jnp.exp2((level - top) * EXP_SCALE)
        return top, one[1] * f1 + f2, one[2] * f1 + out.astype(jnp.float32) * f2

    def local_linear(q, phi_k, v):
        phi_q = feature_map(q)
        affinity = jnp.where(causal, nt(phi_k, phi_q), 0.0).astype(jnp.bfloat16)
        return phi_q, tn(v, affinity)

    def rows_of(h, soft_sum, linear):
        _, total, out = soft_sum
        att = out * (1.0 / total)
        att = att * lax.rsqrt(jnp.mean(att * att, axis=0, keepdims=True) + EPS)
        lin = linear * lax.rsqrt(jnp.mean(linear * linear, axis=0, keepdims=True) + EPS)
        row = att.T * gains[1, pl.ds(h, 1), :] + lin.T * gains[0, pl.ds(h, 1), :]
        return row.astype(jnp.bfloat16)

    def finish(h, soft_sum, linear):
        out_ref[:, cols(h)] = rows_of(h, soft_sum, linear)

    def diagonal(q, k):
        return jnp.where(causal, nt(k, q), LOW)

    def put_state(h, state):
        for i in range(tok // HEAD):
            pack_s[h, HEAD : HEAD + depth, i * HEAD : (i + 1) * HEAD] = state[
                i * depth : (i + 1) * depth
            ].astype(jnp.bfloat16)

    def get_state(h):
        pieces = [
            pack_r[h, HEAD : HEAD + depth, i * HEAD : (i + 1) * HEAD] for i in range(tok // HEAD)
        ]
        return jnp.concatenate(pieces, axis=0)

    def pack_right(h, i, target):
        move(pack_s.at[h], pack_r.at[h], sem_s.at[i], sem_a.at[h], target).start()

    def st_right(h, i, target):
        move(st_s.at[h], st_r.at[h], sem_s.at[i], sem_d.at[h], target).start()

    @pl.when(me == 0)
    def _():
        def start(h):
            for i, src in enumerate((k_ref, v_ref)):
                move(
                    src.at[:, cols(h)], kv0.at[i, :, cols(h)], sem_s.at[0], sem_a.at[h], 1
                ).start()

        each(0, cut, start)
        start(whole)
        each(cut, whole, start)

        wait_loads()

        def compute(h):
            q, k, v = own_qkv(h)
            _, linear = local_linear(q, feature_map(k), v)
            finish(h, soft([diagonal(q, k)], [v]), linear)

        each(0, heads, compute)
        sent(kv0, 0)

    @pl.when(me == 1)
    def _():
        def to_early(i, src, h):
            move(src, early_kv.at[i, h], sem_s.at[0], sem_a.at[h], 2).start()

        def start(h):
            to_early(2, k_ref.at[:, cols(h)], h)
            to_early(3, v_ref.at[:, cols(h)], h)

        each(0, early, start)

        wait_loads()

        def own_rows(h, q, k, v, k0, v0, phi_k, before):
            phi_q, linear = local_linear(q, phi_k, v)
            linear = linear + tt(before.astype(jnp.bfloat16), phi_q)
            finish(h, soft([nt(k0, q), diagonal(q, k)], [v0, v]), linear)

        def early_head(h):
            q, k, v = own_qkv(h)
            arrived(kv0.at[:, :, cols(h)], sem_a.at[h])
            to_early(0, kv0.at[0, :, cols(h)], h)
            to_early(1, kv0.at[1, :, cols(h)], h)
            k0, v0 = kv0[0, :, cols(h)], kv0[1, :, cols(h)]
            before = tn(feature_map(k0), v0)
            own_rows(h, q, k, v, k0, v0, feature_map(k), before)

        each(0, early, early_head)

        def oa_right(h):
            move(oa_s.at[h], oa_r.at[h], sem_s.at[3], sem_b.at[h], 2).start()

        def shared_head(h):
            q, k, v = own_qkv(h)
            phi_k = feature_map(k)
            state = tn(phi_k, v)
            arrived(kv0.at[:, :, cols(h)], sem_a.at[h])
            k0, v0 = kv0[0, :, cols(h)], kv0[1, :, cols(h)]
            before = tn(feature_map(k0), v0)
            put_state(h, before + state)
            arrived(qq.at[:, :, cols(h)], sem_b.at[h])

            def part(i):
                other = qq[i, :, cols(h)]
                level, out = normalised(soft([nt(k0, other), nt(k, other)], [v0, v]))
                st_s[h, i : i + 1] = level
                return out.astype(jnp.bfloat16)

            pack_s[h, :HEAD] = part(1)
            pack_right(h, 1, 2)
            oa_s[h] = part(0)
            st_right(h, 2, 2)

            in_turn(h, oa_right)
            own_rows(h, q, k, v, k0, v0, phi_k, before)

        def whole_head(h):
            q, k, v = own_qkv(h)
            phi_k = feature_map(k)
            arrived(kv0.at[:, :, cols(h)], sem_a.at[h])
            k0, v0 = kv0[0, :, cols(h)], kv0[1, :, cols(h)]
            before = tn(feature_map(k0), v0)
            own_rows(h, q, k, v, k0, v0, phi_k, before)
            before = before + tn(phi_k, v)
            arrived(whole_in, sem_w.at[0])
            q2, k2, v2, q3, k3, v3 = [whole_in[i] for i in range(6)]
            phi_k2 = feature_map(k2)
            after = before + tn(phi_k2, v2)
            phi_q, linear = local_linear(q3, feature_map(k3), v3)
            linear = linear + tt(after.astype(jnp.bfloat16), phi_q)
            scores = [nt(k0, q3), nt(k, q3), nt(k2, q3), diagonal(q3, k3)]
            whole_out[1] = rows_of(h, soft(scores, [v0, v, v2, v3]), linear)
            move(whole_out.at[1], whole_out.at[2], sem_s.at[4], sem_w.at[2], 2).start()
            phi_q, linear = local_linear(q2, phi_k2, v2)
            linear = linear + tt(before.astype(jnp.bfloat16), phi_q)
            scores = [nt(k0, q2), nt(k, q2), diagonal(q2, k2)]
            whole_out[0] = rows_of(h, soft(scores, [v0, v, v2]), linear)

        def head(h):
            @pl.when(h == cut)
            def _():
                whole_head(whole)

            shared_head(h)

        each(early, whole, head)
        each(whole - 2, whole, oa_right)
        move(whole_out.at[0], out_ref.at[:, cols(whole)], sem_s.at[4], sem_w.at[1], 2).start()

        sent(early_kv, 0)
        sent(pack_s.at[early:whole], 1)
        sent(st_s.at[early:whole], 2)
        sent(oa_s.at[early:whole], 3)
        sent(whole_out.at[0:2], 4)

    @pl.when(me == 2)
    def _():
        def to_hub(i, src, dst, h):
            move(src, dst, sem_s.at[0], sem_b.at[h], 1).start()

        def relay(h):
            @pl.when(h == cut)
            def _():
                for i, src in enumerate((q_ref, k_ref, v_ref)):
                    move(
                        src.at[:, cols(whole)], whole_in.at[i], sem_s.at[1], sem_w.at[0], 1
                    ).start()

            q3 = qq.at[1, :, cols(h)]
            to_hub(0, q_ref.at[:, cols(h)], qq.at[0, :, cols(h)], h)
            arrived(q3, sem_c.at[h])
            to_hub(1, q3, q3, h)

        each(early, whole, relay)

        wait_loads()

        def pass_on(h, level, out):
            pack_s[h, :HEAD] = out.astype(jnp.bfloat16)
            st_s[h, 0:1] = level
            st_s[h, 1:2] = level
            pack_right(h, 2, 3)
            st_right(h, 3, 3)

        def early_head(h):
            q, k, v = own_qkv(h)
            arrived(early_kv.at[:, h], sem_a.at[h])
            arrived(qq.at[1, :, cols(h)], sem_c.at[h])
            k0, v0, k1, v1 = [early_kv[i, h] for i in range(4)]
            phi_k = feature_map(k)
            before = tn(feature_map(k0), v0) + tn(feature_map(k1), v1)
            put_state(h, before + tn(phi_k, v))
            q3 = qq[1, :, cols(h)]
            other = soft([nt(k0, q3), nt(k1, q3), nt(k, q3)], [v0, v1, v])
            pass_on(h, *normalised(other))
            phi_q, linear = local_linear(q, phi_k, v)
            linear = linear + tt(before.astype(jnp.bfloat16), phi_q)
            scores = [nt(k0, q), nt(k1, q), diagonal(q, k)]
            finish(h, soft(scores, [v0, v1, v]), linear)

        each(0, early, early_head)

        def for_last(h):
            k, v = own[1, :, cols(h)], own[2, :, cols(h)]
            state = tn(feature_map(k), v)
            other = soft([nt(k, qq[1, :, cols(h)])], [v])
            arrived(pack_r.at[h], sem_a.at[h])
            put_state(h, get_state(h).astype(jnp.float32) + state)
            arrived(st_r.at[h], sem_d.at[h])
            pass_on(h, *normalised(merge(other, st_r[h, 1:2], pack_r[h, :HEAD])))

        def for_own(h):
            q, k, v = own_qkv(h)
            phi_q, linear = local_linear(q, feature_map(k), v)
            linear = linear + tt(get_state(h), phi_q)
            own_sum = soft([diagonal(q, k)], [v])
            arrived(oa_r.at[h], sem_b.at[h])
            finish(h, merge(own_sum, st_r[h, 0:1], oa_r[h]), linear)

        def head(h):
            @pl.when(h == cut)
            def _():
                arrived(whole_out.at[2], sem_w.at[2])
                move(
                    whole_out.at[2], out_ref.at[:, cols(whole)], sem_s.at[4], sem_w.at[1], 3
                ).start()

            for_last(h)
            in_turn(h, for_own)

        each(early, whole, head)
        each(whole - 2, whole, for_own)
        arrived(out_ref.at[:, cols(whole)], sem_w.at[1])

        sent(qq.at[:, :, early * HEAD : whole * HEAD], 0)
        sent(whole_in.at[0:3], 1)
        sent(pack_s.at[0:whole], 2)
        sent(st_s.at[0:whole], 3)
        sent(whole_out.at[2], 4)

    @pl.when(me == 3)
    def _():
        def start(h):
            @pl.when(h == cut)
            def _():
                for i, src in enumerate((q_ref, k_ref, v_ref)):
                    move(
                        src.at[:, cols(whole)], whole_in.at[3 + i], sem_s.at[1], sem_w.at[0], 1
                    ).start()

            move(
                q_ref.at[:, cols(h)], qq.at[1, :, cols(h)], sem_s.at[0], sem_c.at[h], 2
            ).start()

        each(early, whole, start)
        each(0, early, start)

        wait_loads()

        def compute(h):
            q, k, v = own_qkv(h)
            phi_q, linear = local_linear(q, feature_map(k), v)
            own_sum = soft([diagonal(q, k)], [v])
            arrived(pack_r.at[h], sem_a.at[h])
            linear = linear + tt(get_state(h), phi_q)
            arrived(st_r.at[h], sem_d.at[h])
            finish(h, merge(own_sum, st_r[h, 0:1], pack_r[h, :HEAD]), linear)

        each(0, whole, compute)
        arrived(out_ref.at[:, cols(whole)], sem_w.at[1])

        sent(qq.at[1, :, : whole * HEAD], 0)
        sent(whole_in.at[3:6], 1)


def hub_shards(queries, key_vectors, value_vectors, norm_gain, window_gain):
    tok, width = queries.shape
    heads = width // HEAD
    early, _, _ = classes(heads)
    hbm = pl.BlockSpec(memory_space=pl.ANY)
    pack = pltpu.VMEM((heads, HEAD + HEAD * HEAD // tok, tok), jnp.bfloat16)
    partial = pltpu.VMEM((heads, HEAD, tok), jnp.bfloat16)
    stats = pltpu.VMEM((heads, 2, tok), jnp.float32)
    dma = pltpu.SemaphoreType.DMA
    return pl.pallas_call(
        hub_kernel,
        out_shape=pltpu.VMEM((tok, width), jnp.bfloat16),
        in_specs=[hbm] * 5,
        out_specs=pl.BlockSpec(memory_space=pltpu.VMEM),
        scratch_shapes=[
            pltpu.VMEM((2, tok, width), jnp.bfloat16),
            pltpu.VMEM((2, tok, width), jnp.bfloat16),
            pltpu.VMEM((3, tok, width), jnp.bfloat16),
            pltpu.VMEM((2, heads, HEAD), jnp.float32),
            pltpu.VMEM((4, early, tok, HEAD), jnp.bfloat16),
            pltpu.VMEM((6, tok, HEAD), jnp.bfloat16),
            pltpu.VMEM((3, tok, HEAD), jnp.bfloat16),
        ]
        + [pack] * 2
        + [partial] * 2
        + [stats] * 2
        + [dma((heads,))] * 4
        + [dma((3,)), dma((5,)), dma((2,))],
        compiler_params=pltpu.CompilerParams(
            collective_id=0, has_side_effects=True, vmem_limit_bytes=56 * 2**20
        ),
        name="hub_attention",
    )(
        queries,
        key_vectors,
        value_vectors,
        norm_gain.reshape(heads, HEAD),
        window_gain.reshape(heads, HEAD),
    )


def solution(mesh):
    count = mesh.shape["ctx"]

    def run(queries, key_vectors, value_vectors, norm_gain, window_gain):
        args = (queries, key_vectors, value_vectors, norm_gain, window_gain)
        fits = count * queries.shape[0] <= WINDOW
        tok, width = queries.shape
        even = tok % HEAD == 0 and HEAD * HEAD % (16 * tok) == 0
        if fits and even and count == 4 and width >= 8 * HEAD:
            return hub_shards(*args)
        return shards(*args)

    return jax.shard_map(
        run,
        mesh=mesh,
        in_specs=(P(("dp", "ctx"), None), P(("dp", "ctx"), None), P(("dp", "ctx"), None), P(), P()),
        out_specs=P(("dp", "ctx"), None),
        check_vma=False,
    )
```

```python
import functools
import math

import jax
import jax.numpy as jnp
from jax import lax
from jax.experimental import pallas as pl
from jax.experimental.pallas import tpu as pltpu
from jax.sharding import PartitionSpec as P

HEAD = 128
WINDOW = 1024
EPS = 1e-05


def passed_along(value, axis, steps):
    count = lax.axis_size(axis)
    leading, last = (max(0, -steps), min(count, count - steps))
    return lax.ppermute(value, axis, [(source, source + steps) for source in range(leading, last)])


def entering(array, axis, combine, identity):
    peers, position = (lax.axis_size(axis), lax.axis_index(axis))
    everything = lax.all_gather(array.astype(jnp.bfloat16), axis)
    start = jnp.broadcast_to(jnp.asarray(identity, array.dtype), array.shape)

    def lap(k, before):
        reached = k < position
        new = combine(before, everything[k].astype(array.dtype))
        return jnp.where(reached, new, before)

    return lax.fori_loop(0, peers, lap, start)


def feature_map(values):
    upcast = values.astype(jnp.float32)
    return jnp.where(upcast > 0, upcast + 1.0, jnp.exp(jnp.minimum(upcast, 0.0))).astype(
        jnp.bfloat16
    )


def add_states(earlier, later):
    return earlier + later


def shards(queries, key_vectors, value_vectors, norm_gain, window_gain):
    tok_rows, model_width = queries.shape
    head_count = model_width // HEAD
    ctx_index = lax.axis_index("ctx")
    reach_blocks = WINDOW // tok_rows
    own_pair = (key_vectors, value_vectors)
    received = []
    travelling = own_pair
    for distance in range(reach_blocks):
        travelling = passed_along((travelling[0], travelling[1]), "ctx", 1)
        received.append(travelling)
    ordered = received[::-1] + [own_pair]
    window_keys = jnp.concatenate([member[0] for member in ordered], axis=0)
    window_values = jnp.concatenate([member[1] for member in ordered], axis=0)
    span_rows = window_keys.shape[0]
    query_place = ctx_index * tok_rows + jnp.arange(tok_rows, dtype=jnp.int32)
    key_place = (ctx_index - reach_blocks) * tok_rows + jnp.arange(span_rows, dtype=jnp.int32)
    inside = (
        (key_place[None, :] <= query_place[:, None])
        & (query_place[:, None] - key_place[None, :] < WINDOW)
        & (key_place[None, :] >= 0)
    )
    group_size = 4
    groups = head_count // group_size
    scale = 1.0 / math.sqrt(HEAD)

    def split_groups(matrix):
        return jnp.moveaxis(matrix.reshape(matrix.shape[0], groups, group_size, HEAD), 1, 0)

    def attend(operands):
        query_group, key_group, value_group = operands
        scores = (
            jnp.einsum("tge,sge->gts", query_group, key_group, preferred_element_type=jnp.float32)
            * scale
        )
        scores = jnp.where(inside[None], scores, -jnp.inf)
        peak = jnp.max(scores, axis=-1, keepdims=True)
        expos = jnp.exp(scores - peak)
        weights = (expos / jnp.sum(expos, axis=-1, keepdims=True)).astype(jnp.bfloat16)
        return jnp.einsum("gts,sge->tge", weights, value_group, preferred_element_type=jnp.float32)

    attended = lax.map(
        attend, (split_groups(queries), split_groups(window_keys), split_groups(window_values))
    )
    attended = jnp.moveaxis(attended, 0, 1).reshape(tok_rows, head_count, HEAD)
    windowed = attended * lax.rsqrt(jnp.mean(attended * attended, axis=-1, keepdims=True) + EPS)
    windowed = windowed * window_gain.reshape(head_count, HEAD)
    phi_query = feature_map(queries).reshape(tok_rows, head_count, HEAD)
    phi_key = feature_map(key_vectors).reshape(tok_rows, head_count, HEAD)
    value_heads = value_vectors.reshape(tok_rows, head_count, HEAD)
    local_state = jnp.einsum(
        "the,thf->hef", phi_key, value_heads, preferred_element_type=jnp.float32
    )
    carried = entering(local_state, "ctx", add_states, jnp.zeros_like(local_state))
    from_state = jnp.einsum(
        "the,hef->thf", phi_query, carried.astype(jnp.bfloat16), preferred_element_type=jnp.float32
    )
    affinity = jnp.einsum("the,she->hts", phi_query, phi_key, preferred_element_type=jnp.float32)
    inner = jnp.arange(tok_rows, dtype=jnp.int32)
    causal = inner[:, None] >= inner[None, :]
    affinity = jnp.where(causal[None], affinity, 0.0).astype(jnp.bfloat16)
    local_part = jnp.einsum(
        "hts,shf->thf", affinity, value_heads, preferred_element_type=jnp.float32
    )
    linear = from_state + local_part
    normed = linear * lax.rsqrt(jnp.mean(linear * linear, axis=-1, keepdims=True) + EPS)
    normed = normed * norm_gain.reshape(head_count, HEAD)
    return (windowed + normed).reshape(tok_rows, model_width).astype(jnp.bfloat16)


EXP_SCALE = math.log2(math.e) / math.sqrt(HEAD)
LOW = -1e30


def nt(a, b):
    return lax.dot_general(a, b, (((1,), (1,)), ((), ())), preferred_element_type=jnp.float32)


def tn(a, b):
    return lax.dot_general(a, b, (((0,), (0,)), ((), ())), preferred_element_type=jnp.float32)


def tt(a, b):
    return lax.dot_general(a, b, (((0,), (1,)), ((), ())), preferred_element_type=jnp.float32)


def classes(heads):
    return heads // 8, heads // 16, heads // 2, heads - 1


def hub_kernel(
    q_ref, k_ref, v_ref, gn_ref, gw_ref, out_ref,
    kv0, qq, own, gains, early_kv, whole_in, whole_out, pack_s, pack_r, oa_s, oa_r, st_s, st_r,
    sem_a, sem_b, sem_c, sem_d, sem_w, sem_s, loaded,
):
    tok, width = q_ref.shape
    heads = width // HEAD
    most, least, cut, whole = classes(heads)
    depth = HEAD * HEAD // tok
    me = lax.axis_index("ctx")
    fewer = lax.rem(lax.axis_index("dp"), 2)
    early = most + fewer * (least - most)
    direct = 2
    turn = 8
    lag = 3
    MESH = pl.DeviceIdType.MESH

    def cols(h):
        if isinstance(h, int):
            return pl.ds(h * HEAD, HEAD)
        return pl.ds(pl.multiple_of(h * HEAD, HEAD), HEAD)

    def move(src, dst, sent, arrived, target):
        return pltpu.make_async_remote_copy(
            src_ref=src,
            dst_ref=dst,
            send_sem=sent,
            recv_sem=arrived,
            device_id={"ctx": target},
            device_id_type=MESH,
        )

    def arrived(ref, sem):
        move(ref, ref, sem_s.at[0], sem, 0).wait_recv()

    def sent(ref, i):
        move(ref, ref, sem_s.at[i], sem_w.at[0], 0).wait_send()

    def each(start, stop, body):
        def step(h, carry):
            body(h)
            return carry

        lax.fori_loop(start, stop, step, 0)

    def by_early(body):
        for which, count in enumerate((most, least)):

            @pl.when(fewer == which)
            def _():
                body(count)

    skips = [cut + 2 * i for i in range(lag)]

    def in_turn(h, body):
        late = sum((h >= at).astype(jnp.int32) for at in skips)

        @pl.when(functools.reduce(jnp.logical_and, [h != at for at in skips]))
        def _():
            body(h - late)

    loads = [
        pltpu.make_async_copy(src, own.at[i], loaded.at[0])
        for i, src in enumerate([q_ref, k_ref, v_ref])
    ] + [
        pltpu.make_async_copy(src, gains.at[i], loaded.at[1])
        for i, src in enumerate([gn_ref, gw_ref])
    ]
    for load in loads:
        load.start()

    def wait_loads():
        pltpu.make_async_copy(own, own, loaded.at[0]).wait()
        pltpu.make_async_copy(gains, gains, loaded.at[1]).wait()

    barrier = pltpu.get_barrier_semaphore()
    senders = {1: (0, 2, 3), 2: (1, 3)}
    for device, others in senders.items():

        @pl.when(me == device)
        def _():
            for other in others:
                pl.semaphore_signal(
                    barrier, inc=1, device_id={"ctx": other}, device_id_type=MESH
                )

    pl.semaphore_wait(barrier, 1 + (me == 3).astype(jnp.int32))

    key_at = lax.broadcasted_iota(jnp.int32, (tok, tok), 0)
    query_at = lax.broadcasted_iota(jnp.int32, (tok, tok), 1)
    causal = key_at <= query_at

    def own_qkv(h):
        return own[0, :, cols(h)], own[1, :, cols(h)], own[2, :, cols(h)]

    def soft(scores, values):
        peak = functools.reduce(
            jnp.maximum, [jnp.max(s, axis=0, keepdims=True) for s in scores]
        )
        total, out = 0.0, 0.0
        for s, v in zip(scores, values):
            e = jnp.exp2((s - peak) * EXP_SCALE)
            total = total + jnp.sum(e, axis=0, keepdims=True)
            out = out + tn(v, e.astype(jnp.bfloat16))
        return peak, total, out

    def normalised(soft_sum):
        peak, total, out = soft_sum
        return peak + jnp.log2(total) * (1.0 / EXP_SCALE), out * (1.0 / total)

    def merge(one, level, out):
        top = jnp.maximum(one[0], level)
        f1 = jnp.exp2((one[0] - top) * EXP_SCALE)
        f2 = jnp.exp2((level - top) * EXP_SCALE)
        return top, one[1] * f1 + f2, one[2] * f1 + out.astype(jnp.float32) * f2

    def local_linear(q, phi_k, v):
        phi_q = feature_map(q)
        affinity = jnp.where(causal, nt(phi_k, phi_q), 0.0).astype(jnp.bfloat16)
        return phi_q, tn(v, affinity)

    def rows_of(h, soft_sum, linear):
        _, total, out = soft_sum
        att = out * (1.0 / total)
        att = att * lax.rsqrt(jnp.mean(att * att, axis=0, keepdims=True) + EPS)
        lin = linear * lax.rsqrt(jnp.mean(linear * linear, axis=0, keepdims=True) + EPS)
        row = att.T * gains[1, pl.ds(h, 1), :] + lin.T * gains[0, pl.ds(h, 1), :]
        return row.astype(jnp.bfloat16)

    def finish(h, soft_sum, linear):
        out_ref[:, cols(h)] = rows_of(h, soft_sum, linear)

    def diagonal(q, k):
        return jnp.where(causal, nt(k, q), LOW)

    def put_state(h, state):
        for i in range(tok // HEAD):
            pack_s[h, HEAD : HEAD + depth, i * HEAD : (i + 1) * HEAD] = state[
                i * depth : (i + 1) * depth
            ].astype(jnp.bfloat16)

    def get_state(h):
        pieces = [
            pack_r[h, HEAD : HEAD + depth, i * HEAD : (i + 1) * HEAD] for i in range(tok // HEAD)
        ]
        return jnp.concatenate(pieces, axis=0)

    def pack_right(h, i, target):
        move(pack_s.at[h], pack_r.at[h], sem_s.at[i], sem_a.at[h], target).start()

    def st_right(h, i, target):
        move(st_s.at[h], st_r.at[h], sem_s.at[i], sem_d.at[h], target).start()

    @pl.when(me == 0)
    def _():
        def start(h):
            for i, src in enumerate((k_ref, v_ref)):
                move(
                    src.at[:, cols(h)], kv0.at[i, :, cols(h)], sem_s.at[0], sem_a.at[h], 1
                ).start()

        each(0, heads, start)

        wait_loads()

        def compute(h):
            q, k, v = own_qkv(h)
            _, linear = local_linear(q, feature_map(k), v)
            finish(h, soft([diagonal(q, k)], [v]), linear)

        each(0, heads, compute)
        sent(kv0, 0)

    @pl.when(me == 1)
    def _():
        def to_early(i, src, h):
            move(src, early_kv.at[i, h], sem_s.at[0], sem_a.at[h], 2).start()

        def start(h):
            to_early(2, k_ref.at[:, cols(h)], h)
            to_early(3, v_ref.at[:, cols(h)], h)

        each(0, early, start)

        wait_loads()

        def own_rows(h, q, k, v, k0, v0, phi_k, before):
            phi_q, linear = local_linear(q, phi_k, v)
            linear = linear + tt(before.astype(jnp.bfloat16), phi_q)
            finish(h, soft([nt(k0, q), diagonal(q, k)], [v0, v]), linear)

        def early_head(h):
            q, k, v = own_qkv(h)
            arrived(kv0.at[:, :, cols(h)], sem_a.at[h])
            to_early(0, kv0.at[0, :, cols(h)], h)
            to_early(1, kv0.at[1, :, cols(h)], h)
            k0, v0 = kv0[0, :, cols(h)], kv0[1, :, cols(h)]
            before = tn(feature_map(k0), v0)
            own_rows(h, q, k, v, k0, v0, feature_map(k), before)

        each(0, early, early_head)

        def oa_right(h):
            move(oa_s.at[h], oa_r.at[h], sem_s.at[3], sem_b.at[h], 2).start()

        def shared_head(h):
            q, k, v = own_qkv(h)
            phi_k = feature_map(k)
            state = tn(phi_k, v)
            arrived(kv0.at[:, :, cols(h)], sem_a.at[h])
            k0, v0 = kv0[0, :, cols(h)], kv0[1, :, cols(h)]
            before = tn(feature_map(k0), v0)
            put_state(h, before + state)
            arrived(qq.at[:, :, cols(h)], sem_b.at[h])

            def part(i):
                other = qq[i, :, cols(h)]
                level, out = normalised(soft([nt(k0, other), nt(k, other)], [v0, v]))
                st_s[h, i : i + 1] = level
                return out.astype(jnp.bfloat16)

            pack_s[h, :HEAD] = part(1)
            pack_right(h, 1, 2)
            oa_s[h] = part(0)
            st_right(h, 2, 2)

            in_turn(h, oa_right)
            own_rows(h, q, k, v, k0, v0, phi_k, before)

        def out_right(i, target):
            move(
                whole_out.at[i], out_ref.at[:, cols(whole)], sem_s.at[4], sem_w.at[1], target
            ).start()

        def whole_head(h):
            q, k, v = own_qkv(h)
            phi_k = feature_map(k)
            arrived(kv0.at[:, :, cols(h)], sem_a.at[h])
            k0, v0 = kv0[0, :, cols(h)], kv0[1, :, cols(h)]
            before = tn(feature_map(k0), v0)
            own_rows(h, q, k, v, k0, v0, phi_k, before)
            before = before + tn(phi_k, v)
            arrived(whole_in, sem_w.at[0])
            q2, k2, v2, q3, k3, v3 = [whole_in[i] for i in range(6)]
            phi_k2 = feature_map(k2)
            after = before + tn(phi_k2, v2)
            phi_q, linear = local_linear(q3, feature_map(k3), v3)
            linear = linear + tt(after.astype(jnp.bfloat16), phi_q)
            scores = [nt(k0, q3), nt(k, q3), nt(k2, q3), diagonal(q3, k3)]
            whole_out[1] = rows_of(h, soft(scores, [v0, v, v2, v3]), linear)
            out_right(1, 3)
            phi_q, linear = local_linear(q2, phi_k2, v2)
            linear = linear + tt(before.astype(jnp.bfloat16), phi_q)
            scores = [nt(k0, q2), nt(k, q2), diagonal(q2, k2)]
            whole_out[0] = rows_of(h, soft(scores, [v0, v, v2]), linear)
            out_right(0, 2)

        each(early, whole, shared_head)
        each(whole - lag, whole, oa_right)
        whole_head(whole)

        def drain(count):
            sent(early_kv.at[:, 0:count], 0)
            sent(pack_s.at[count:whole], 1)
            sent(st_s.at[count:whole], 2)
            sent(oa_s.at[count:whole], 3)

        by_early(drain)
        sent(whole_out, 4)

    @pl.when(me == 2)
    def _():
        def start(h):
            move(
                q_ref.at[:, cols(h)], qq.at[0, :, cols(h)], sem_s.at[0], sem_b.at[h], 1
            ).start()

        def relay(h):
            start(h)
            q3 = qq.at[1, :, cols(h)]
            arrived(q3, sem_c.at[h])
            move(q3, q3, sem_s.at[5], sem_b.at[h], 1).start()

        each(early, early + direct, start)
        each(early + direct, whole, relay)
        for i, src in enumerate((q_ref, k_ref, v_ref)):
            move(src.at[:, cols(whole)], whole_in.at[i], sem_s.at[1], sem_w.at[0], 1).start()

        wait_loads()

        def pass_on(h, level, out):
            pack_s[h, :HEAD] = out.astype(jnp.bfloat16)
            st_s[h, 0:1] = level
            st_s[h, 1:2] = level
            pack_right(h, 2, 3)
            st_right(h, 3, 3)

        def early_head(h):
            q, k, v = own_qkv(h)
            arrived(early_kv.at[:, h], sem_a.at[h])
            arrived(qq.at[1, :, cols(h)], sem_c.at[h])
            k0, v0, k1, v1 = [early_kv[i, h] for i in range(4)]
            phi_k = feature_map(k)
            before = tn(feature_map(k0), v0) + tn(feature_map(k1), v1)
            put_state(h, before + tn(phi_k, v))
            q3 = qq[1, :, cols(h)]
            other = soft([nt(k0, q3), nt(k1, q3), nt(k, q3)], [v0, v1, v])
            pass_on(h, *normalised(other))
            phi_q, linear = local_linear(q, phi_k, v)
            linear = linear + tt(before.astype(jnp.bfloat16), phi_q)
            scores = [nt(k0, q), nt(k1, q), diagonal(q, k)]
            finish(h, soft(scores, [v0, v1, v]), linear)

        each(0, early, early_head)

        def for_last(h):
            k, v = own[1, :, cols(h)], own[2, :, cols(h)]
            state = tn(feature_map(k), v)

            @pl.when(h < early + direct)
            def _():
                arrived(qq.at[1, :, cols(h)], sem_c.at[h])

            other = soft([nt(k, qq[1, :, cols(h)])], [v])
            arrived(pack_r.at[h], sem_a.at[h])
            put_state(h, get_state(h).astype(jnp.float32) + state)
            arrived(st_r.at[h], sem_d.at[h])
            pass_on(h, *normalised(merge(other, st_r[h, 1:2], pack_r[h, :HEAD])))

        def for_own(h):
            q, k, v = own_qkv(h)
            phi_q, linear = local_linear(q, feature_map(k), v)
            linear = linear + tt(get_state(h), phi_q)
            own_sum = soft([diagonal(q, k)], [v])
            arrived(oa_r.at[h], sem_b.at[h])
            finish(h, merge(own_sum, st_r[h, 0:1], oa_r[h]), linear)

        def head(h):
            for_last(h)
            in_turn(h, for_own)

        each(early, whole, head)
        each(whole - lag, whole, for_own)
        arrived(out_ref.at[:, cols(whole)], sem_w.at[1])


        def drain(count):
            sent(qq.at[0, :, count * HEAD : whole * HEAD], 0)
            sent(qq.at[1, :, (count + direct) * HEAD : whole * HEAD], 5)

        by_early(drain)
        sent(whole_in.at[0:3], 1)
        sent(pack_s.at[0:whole], 2)
        sent(st_s.at[0:whole], 3)

    @pl.when(me == 3)
    def _():
        def to_hub(h):
            move(
                q_ref.at[:, cols(h)], qq.at[1, :, cols(h)], sem_s.at[2], sem_b.at[h], 1
            ).start()

        def to_left(h):
            move(
                q_ref.at[:, cols(h)], qq.at[1, :, cols(h)], sem_s.at[0], sem_c.at[h], 2
            ).start()

        each(early, early + direct, to_hub)
        each(early + direct, whole, to_left)
        each(0, early + direct, to_left)

        wait_loads()

        def compute(h):
            q, k, v = own_qkv(h)
            phi_q, linear = local_linear(q, feature_map(k), v)
            own_sum = soft([diagonal(q, k)], [v])
            arrived(pack_r.at[h], sem_a.at[h])
            linear = linear + tt(get_state(h), phi_q)
            arrived(st_r.at[h], sem_d.at[h])
            finish(h, merge(own_sum, st_r[h, 0:1], pack_r[h, :HEAD]), linear)

        each(0, turn, compute)
        for i, src in enumerate((q_ref, k_ref, v_ref)):
            move(src.at[:, cols(whole)], whole_in.at[3 + i], sem_s.at[1], sem_w.at[0], 1).start()
        each(turn, whole, compute)
        arrived(out_ref.at[:, cols(whole)], sem_w.at[1])

        sent(qq.at[1, :, : whole * HEAD], 0)
        sent(whole_in.at[3:6], 1)
        by_early(lambda count: sent(qq.at[1, :, count * HEAD : (count + direct) * HEAD], 2))


def hub_shards(queries, key_vectors, value_vectors, norm_gain, window_gain):
    tok, width = queries.shape
    heads = width // HEAD
    most = classes(heads)[0]
    hbm = pl.BlockSpec(memory_space=pl.ANY)
    pack = pltpu.VMEM((heads, HEAD + HEAD * HEAD // tok, tok), jnp.bfloat16)
    partial = pltpu.VMEM((heads, HEAD, tok), jnp.bfloat16)
    stats = pltpu.VMEM((heads, 2, tok), jnp.float32)
    dma = pltpu.SemaphoreType.DMA
    return pl.pallas_call(
        hub_kernel,
        out_shape=pltpu.VMEM((tok, width), jnp.bfloat16),
        in_specs=[hbm] * 5,
        out_specs=pl.BlockSpec(memory_space=pltpu.VMEM),
        scratch_shapes=[
            pltpu.VMEM((2, tok, width), jnp.bfloat16),
            pltpu.VMEM((2, tok, width), jnp.bfloat16),
            pltpu.VMEM((3, tok, width), jnp.bfloat16),
            pltpu.VMEM((2, heads, HEAD), jnp.float32),
            pltpu.VMEM((4, most, tok, HEAD), jnp.bfloat16),
            pltpu.VMEM((6, tok, HEAD), jnp.bfloat16),
            pltpu.VMEM((2, tok, HEAD), jnp.bfloat16),
        ]
        + [pack] * 2
        + [partial] * 2
        + [stats] * 2
        + [dma((heads,))] * 4
        + [dma((2,)), dma((6,)), dma((2,))],
        compiler_params=pltpu.CompilerParams(
            collective_id=0, has_side_effects=True, vmem_limit_bytes=56 * 2**20
        ),
        name="hub_attention",
    )(
        queries,
        key_vectors,
        value_vectors,
        norm_gain.reshape(heads, HEAD),
        window_gain.reshape(heads, HEAD),
    )


def solution(mesh):
    count = mesh.shape["ctx"]

    def run(queries, key_vectors, value_vectors, norm_gain, window_gain):
        args = (queries, key_vectors, value_vectors, norm_gain, window_gain)
        fits = count * queries.shape[0] <= WINDOW
        tok, width = queries.shape
        even = tok % HEAD == 0 and HEAD * HEAD % (16 * tok) == 0
        if fits and even and count == 4 and width >= 16 * HEAD:
            return hub_shards(*args)
        return shards(*args)

    return jax.shard_map(
        run,
        mesh=mesh,
        in_specs=(P(("dp", "ctx"), None), P(("dp", "ctx"), None), P(("dp", "ctx"), None), P(), P()),
        out_specs=P(("dp", "ctx"), None),
        check_vma=False,
    )
```

```python
import functools
import math

import jax
import jax.numpy as jnp
from jax import lax
from jax.experimental import pallas as pl
from jax.experimental.pallas import tpu as pltpu
from jax.sharding import PartitionSpec as P

HEAD = 128
WINDOW = 1024
EPS = 1e-05


def passed_along(value, axis, steps):
    count = lax.axis_size(axis)
    leading, last = (max(0, -steps), min(count, count - steps))
    return lax.ppermute(value, axis, [(source, source + steps) for source in range(leading, last)])


def entering(array, axis, combine, identity):
    peers, position = (lax.axis_size(axis), lax.axis_index(axis))
    everything = lax.all_gather(array.astype(jnp.bfloat16), axis)
    start = jnp.broadcast_to(jnp.asarray(identity, array.dtype), array.shape)

    def lap(k, before):
        reached = k < position
        new = combine(before, everything[k].astype(array.dtype))
        return jnp.where(reached, new, before)

    return lax.fori_loop(0, peers, lap, start)


def feature_map(values):
    upcast = values.astype(jnp.float32)
    return jnp.where(upcast > 0, upcast + 1.0, jnp.exp(jnp.minimum(upcast, 0.0))).astype(
        jnp.bfloat16
    )


def add_states(earlier, later):
    return earlier + later


def shards(queries, key_vectors, value_vectors, norm_gain, window_gain):
    tok_rows, model_width = queries.shape
    head_count = model_width // HEAD
    ctx_index = lax.axis_index("ctx")
    reach_blocks = WINDOW // tok_rows
    own_pair = (key_vectors, value_vectors)
    received = []
    travelling = own_pair
    for distance in range(reach_blocks):
        travelling = passed_along((travelling[0], travelling[1]), "ctx", 1)
        received.append(travelling)
    ordered = received[::-1] + [own_pair]
    window_keys = jnp.concatenate([member[0] for member in ordered], axis=0)
    window_values = jnp.concatenate([member[1] for member in ordered], axis=0)
    span_rows = window_keys.shape[0]
    query_place = ctx_index * tok_rows + jnp.arange(tok_rows, dtype=jnp.int32)
    key_place = (ctx_index - reach_blocks) * tok_rows + jnp.arange(span_rows, dtype=jnp.int32)
    inside = (
        (key_place[None, :] <= query_place[:, None])
        & (query_place[:, None] - key_place[None, :] < WINDOW)
        & (key_place[None, :] >= 0)
    )
    group_size = 4
    groups = head_count // group_size
    scale = 1.0 / math.sqrt(HEAD)

    def split_groups(matrix):
        return jnp.moveaxis(matrix.reshape(matrix.shape[0], groups, group_size, HEAD), 1, 0)

    def attend(operands):
        query_group, key_group, value_group = operands
        scores = (
            jnp.einsum("tge,sge->gts", query_group, key_group, preferred_element_type=jnp.float32)
            * scale
        )
        scores = jnp.where(inside[None], scores, -jnp.inf)
        peak = jnp.max(scores, axis=-1, keepdims=True)
        expos = jnp.exp(scores - peak)
        weights = (expos / jnp.sum(expos, axis=-1, keepdims=True)).astype(jnp.bfloat16)
        return jnp.einsum("gts,sge->tge", weights, value_group, preferred_element_type=jnp.float32)

    attended = lax.map(
        attend, (split_groups(queries), split_groups(window_keys), split_groups(window_values))
    )
    attended = jnp.moveaxis(attended, 0, 1).reshape(tok_rows, head_count, HEAD)
    windowed = attended * lax.rsqrt(jnp.mean(attended * attended, axis=-1, keepdims=True) + EPS)
    windowed = windowed * window_gain.reshape(head_count, HEAD)
    phi_query = feature_map(queries).reshape(tok_rows, head_count, HEAD)
    phi_key = feature_map(key_vectors).reshape(tok_rows, head_count, HEAD)
    value_heads = value_vectors.reshape(tok_rows, head_count, HEAD)
    local_state = jnp.einsum(
        "the,thf->hef", phi_key, value_heads, preferred_element_type=jnp.float32
    )
    carried = entering(local_state, "ctx", add_states, jnp.zeros_like(local_state))
    from_state = jnp.einsum(
        "the,hef->thf", phi_query, carried.astype(jnp.bfloat16), preferred_element_type=jnp.float32
    )
    affinity = jnp.einsum("the,she->hts", phi_query, phi_key, preferred_element_type=jnp.float32)
    inner = jnp.arange(tok_rows, dtype=jnp.int32)
    causal = inner[:, None] >= inner[None, :]
    affinity = jnp.where(causal[None], affinity, 0.0).astype(jnp.bfloat16)
    local_part = jnp.einsum(
        "hts,shf->thf", affinity, value_heads, preferred_element_type=jnp.float32
    )
    linear = from_state + local_part
    normed = linear * lax.rsqrt(jnp.mean(linear * linear, axis=-1, keepdims=True) + EPS)
    normed = normed * norm_gain.reshape(head_count, HEAD)
    return (windowed + normed).reshape(tok_rows, model_width).astype(jnp.bfloat16)


EXP_SCALE = math.log2(math.e) / math.sqrt(HEAD)
LOW = -1e30


def nt(a, b):
    return lax.dot_general(a, b, (((1,), (1,)), ((), ())), preferred_element_type=jnp.float32)


def tn(a, b):
    return lax.dot_general(a, b, (((0,), (0,)), ((), ())), preferred_element_type=jnp.float32)


def tt(a, b):
    return lax.dot_general(a, b, (((0,), (1,)), ((), ())), preferred_element_type=jnp.float32)


def classes(heads):
    return heads // 8, heads // 16, heads // 2, heads - heads // 8


def hub_kernel(
    q_ref, k_ref, v_ref, gn_ref, gw_ref, out_ref,
    kv0, qq, own, gains, early_kv, whole_in, whole_out, pack_s, pack_r, oa_s, oa_r, st_s, st_r,
    sem_a, sem_b, sem_c, sem_d, sem_w, sem_s, loaded,
):
    tok, width = q_ref.shape
    heads = width // HEAD
    most, least, cut, whole = classes(heads)
    count = heads - whole
    depth = HEAD * HEAD // tok
    me = lax.axis_index("ctx")
    fewer = lax.rem(lax.axis_index("dp"), 2)
    early = most + fewer * (least - most)
    direct = 2
    turn = 7
    lag = 2
    MESH = pl.DeviceIdType.MESH

    def cols(h):
        if isinstance(h, int):
            return pl.ds(h * HEAD, HEAD)
        return pl.ds(pl.multiple_of(h * HEAD, HEAD), HEAD)

    def move(src, dst, sent, arrived, target):
        return pltpu.make_async_remote_copy(
            src_ref=src,
            dst_ref=dst,
            send_sem=sent,
            recv_sem=arrived,
            device_id={"ctx": target},
            device_id_type=MESH,
        )

    def arrived(ref, sem):
        move(ref, ref, sem_s.at[0], sem, 0).wait_recv()

    def sent(ref, i):
        move(ref, ref, sem_s.at[i], sem_w.at[0], 0).wait_send()

    def to_whole(c, i, src, sem):
        move(
            src.at[:, cols(whole + c)], whole_in.at[c, i], sem_s.at[1], sem_w.at[sem], 1
        ).start()

    def each(start, stop, body):
        def step(h, carry):
            body(h)
            return carry

        lax.fori_loop(start, stop, step, 0)

    def by_early(body):
        for which, count in enumerate((most, least)):

            @pl.when(fewer == which)
            def _():
                body(count)

    skips = [cut + 2 * i for i in range(lag)]

    def in_turn(h, body):
        late = sum((h >= at).astype(jnp.int32) for at in skips)

        @pl.when(functools.reduce(jnp.logical_and, [h != at for at in skips]))
        def _():
            body(h - late)

    loads = [
        pltpu.make_async_copy(src, own.at[i], loaded.at[0])
        for i, src in enumerate([q_ref, k_ref, v_ref])
    ] + [
        pltpu.make_async_copy(src, gains.at[i], loaded.at[1])
        for i, src in enumerate([gn_ref, gw_ref])
    ]
    for load in loads:
        load.start()

    def wait_loads():
        pltpu.make_async_copy(own, own, loaded.at[0]).wait()
        pltpu.make_async_copy(gains, gains, loaded.at[1]).wait()

    barrier = pltpu.get_barrier_semaphore()
    senders = {1: (0, 2, 3), 2: (1, 3)}
    for device, others in senders.items():

        @pl.when(me == device)
        def _():
            for other in others:
                pl.semaphore_signal(
                    barrier, inc=1, device_id={"ctx": other}, device_id_type=MESH
                )

    pl.semaphore_wait(barrier, 1 + (me == 3).astype(jnp.int32))

    key_at = lax.broadcasted_iota(jnp.int32, (tok, tok), 0)
    query_at = lax.broadcasted_iota(jnp.int32, (tok, tok), 1)
    causal = key_at <= query_at

    def own_qkv(h):
        return own[0, :, cols(h)], own[1, :, cols(h)], own[2, :, cols(h)]

    def soft(scores, values):
        peak = functools.reduce(
            jnp.maximum, [jnp.max(s, axis=0, keepdims=True) for s in scores]
        )
        total, out = 0.0, 0.0
        for s, v in zip(scores, values):
            e = jnp.exp2((s - peak) * EXP_SCALE)
            total = total + jnp.sum(e, axis=0, keepdims=True)
            out = out + tn(v, e.astype(jnp.bfloat16))
        return peak, total, out

    def normalised(soft_sum):
        peak, total, out = soft_sum
        return peak + jnp.log2(total) * (1.0 / EXP_SCALE), out * (1.0 / total)

    def merge(one, level, out):
        top = jnp.maximum(one[0], level)
        f1 = jnp.exp2((one[0] - top) * EXP_SCALE)
        f2 = jnp.exp2((level - top) * EXP_SCALE)
        return top, one[1] * f1 + f2, one[2] * f1 + out.astype(jnp.float32) * f2

    def local_linear(q, phi_k, v):
        phi_q = feature_map(q)
        affinity = jnp.where(causal, nt(phi_k, phi_q), 0.0).astype(jnp.bfloat16)
        return phi_q, tn(v, affinity)

    def rows_of(h, soft_sum, linear):
        _, total, out = soft_sum
        att = out * (1.0 / total)
        att = att * lax.rsqrt(jnp.mean(att * att, axis=0, keepdims=True) + EPS)
        lin = linear * lax.rsqrt(jnp.mean(linear * linear, axis=0, keepdims=True) + EPS)
        row = att.T * gains[1, pl.ds(h, 1), :] + lin.T * gains[0, pl.ds(h, 1), :]
        return row.astype(jnp.bfloat16)

    def finish(h, soft_sum, linear):
        out_ref[:, cols(h)] = rows_of(h, soft_sum, linear)

    def diagonal(q, k):
        return jnp.where(causal, nt(k, q), LOW)

    def put_state(h, state):
        for i in range(tok // HEAD):
            pack_s[h, HEAD : HEAD + depth, i * HEAD : (i + 1) * HEAD] = state[
                i * depth : (i + 1) * depth
            ].astype(jnp.bfloat16)

    def get_state(h):
        pieces = [
            pack_r[h, HEAD : HEAD + depth, i * HEAD : (i + 1) * HEAD] for i in range(tok // HEAD)
        ]
        return jnp.concatenate(pieces, axis=0)

    def pack_right(h, i, target):
        move(pack_s.at[h], pack_r.at[h], sem_s.at[i], sem_a.at[h], target).start()

    def st_right(h, i, target):
        move(st_s.at[h], st_r.at[h], sem_s.at[i], sem_d.at[h], target).start()

    @pl.when(me == 0)
    def _():
        def start(h):
            for i, src in enumerate((k_ref, v_ref)):
                move(
                    src.at[:, cols(h)], kv0.at[i, :, cols(h)], sem_s.at[0], sem_a.at[h], 1
                ).start()

        each(0, heads, start)

        wait_loads()

        def compute(h):
            q, k, v = own_qkv(h)
            _, linear = local_linear(q, feature_map(k), v)
            finish(h, soft([diagonal(q, k)], [v]), linear)

        each(0, heads, compute)
        sent(kv0, 0)

    @pl.when(me == 1)
    def _():
        def to_early(i, src, h):
            move(src, early_kv.at[i, h], sem_s.at[0], sem_a.at[h], 2).start()

        def start(h):
            to_early(2, k_ref.at[:, cols(h)], h)
            to_early(3, v_ref.at[:, cols(h)], h)

        each(0, early, start)

        wait_loads()

        def own_rows(h, q, k, v, k0, v0, phi_k, before):
            phi_q, linear = local_linear(q, phi_k, v)
            linear = linear + tt(before.astype(jnp.bfloat16), phi_q)
            finish(h, soft([nt(k0, q), diagonal(q, k)], [v0, v]), linear)

        def early_head(h):
            q, k, v = own_qkv(h)
            arrived(kv0.at[:, :, cols(h)], sem_a.at[h])
            to_early(0, kv0.at[0, :, cols(h)], h)
            to_early(1, kv0.at[1, :, cols(h)], h)
            k0, v0 = kv0[0, :, cols(h)], kv0[1, :, cols(h)]
            before = tn(feature_map(k0), v0)
            own_rows(h, q, k, v, k0, v0, feature_map(k), before)

        each(0, early, early_head)

        def oa_right(h):
            move(oa_s.at[h], oa_r.at[h], sem_s.at[3], sem_b.at[h], 2).start()

        def shared_head(h):
            q, k, v = own_qkv(h)
            phi_k = feature_map(k)
            state = tn(phi_k, v)
            arrived(kv0.at[:, :, cols(h)], sem_a.at[h])
            k0, v0 = kv0[0, :, cols(h)], kv0[1, :, cols(h)]
            before = tn(feature_map(k0), v0)
            put_state(h, before + state)
            arrived(qq.at[:, :, cols(h)], sem_b.at[h])

            def part(i):
                other = qq[i, :, cols(h)]
                level, out = normalised(soft([nt(k0, other), nt(k, other)], [v0, v]))
                st_s[h, i : i + 1] = level
                return out.astype(jnp.bfloat16)

            pack_s[h, :HEAD] = part(1)
            pack_right(h, 1, 2)
            oa_s[h] = part(0)
            st_right(h, 2, 2)

            in_turn(h, oa_right)
            own_rows(h, q, k, v, k0, v0, phi_k, before)

        def out_right(c, i, target):
            move(
                whole_out.at[c, i],
                out_ref.at[:, cols(whole + c)],
                sem_s.at[4],
                sem_w.at[2 * count],
                target,
            ).start()

        def whole_head(c):
            h = whole + c
            q, k, v = own_qkv(h)
            phi_k = feature_map(k)
            arrived(kv0.at[:, :, cols(h)], sem_a.at[h])
            k0, v0 = kv0[0, :, cols(h)], kv0[1, :, cols(h)]
            before = tn(feature_map(k0), v0)
            own_rows(h, q, k, v, k0, v0, phi_k, before)
            before = before + tn(phi_k, v)
            arrived(whole_in.at[c, 0:5], sem_w.at[c])
            k2, v2, q3, k3, v3 = [whole_in[c, i] for i in range(5)]
            phi_k2 = feature_map(k2)
            after = before + tn(phi_k2, v2)
            phi_q, linear = local_linear(q3, feature_map(k3), v3)
            linear = linear + tt(after.astype(jnp.bfloat16), phi_q)
            scores = [nt(k0, q3), nt(k, q3), nt(k2, q3), diagonal(q3, k3)]
            whole_out[c, 1] = rows_of(h, soft(scores, [v0, v, v2, v3]), linear)
            out_right(c, 1, 3)
            arrived(whole_in.at[c, 5], sem_w.at[count + c])
            q2 = whole_in[c, 5]
            phi_q, linear = local_linear(q2, phi_k2, v2)
            linear = linear + tt(before.astype(jnp.bfloat16), phi_q)
            scores = [nt(k0, q2), nt(k, q2), diagonal(q2, k2)]
            whole_out[c, 0] = rows_of(h, soft(scores, [v0, v, v2]), linear)
            out_right(c, 0, 2)

        each(early, whole, shared_head)
        each(whole - lag, whole, oa_right)
        each(0, count, whole_head)

        def drain(count):
            sent(early_kv.at[:, 0:count], 0)
            sent(pack_s.at[count:whole], 1)
            sent(st_s.at[count:whole], 2)
            sent(oa_s.at[count:whole], 3)

        by_early(drain)
        sent(whole_out, 4)

    @pl.when(me == 2)
    def _():
        def start(h):
            move(
                q_ref.at[:, cols(h)], qq.at[0, :, cols(h)], sem_s.at[0], sem_b.at[h], 1
            ).start()

        def relay(h):
            start(h)
            q3 = qq.at[1, :, cols(h)]
            arrived(q3, sem_c.at[h])
            move(q3, q3, sem_s.at[5], sem_b.at[h], 1).start()

        each(early, early + direct, start)
        each(early + direct, whole, relay)
        for c in range(count):
            for i, src, sem in ((0, k_ref, c), (1, v_ref, c), (5, q_ref, count + c)):
                to_whole(c, i, src, sem)

        wait_loads()

        def pass_on(h, level, out):
            pack_s[h, :HEAD] = out.astype(jnp.bfloat16)
            st_s[h, 0:1] = level
            st_s[h, 1:2] = level
            pack_right(h, 2, 3)
            st_right(h, 3, 3)

        def early_head(h):
            q, k, v = own_qkv(h)
            arrived(early_kv.at[:, h], sem_a.at[h])
            arrived(qq.at[1, :, cols(h)], sem_c.at[h])
            k0, v0, k1, v1 = [early_kv[i, h] for i in range(4)]
            phi_k = feature_map(k)
            before = tn(feature_map(k0), v0) + tn(feature_map(k1), v1)
            put_state(h, before + tn(phi_k, v))
            q3 = qq[1, :, cols(h)]
            other = soft([nt(k0, q3), nt(k1, q3), nt(k, q3)], [v0, v1, v])
            pass_on(h, *normalised(other))
            phi_q, linear = local_linear(q, phi_k, v)
            linear = linear + tt(before.astype(jnp.bfloat16), phi_q)
            scores = [nt(k0, q), nt(k1, q), diagonal(q, k)]
            finish(h, soft(scores, [v0, v1, v]), linear)

        each(0, early, early_head)

        def for_last(h):
            k, v = own[1, :, cols(h)], own[2, :, cols(h)]
            state = tn(feature_map(k), v)

            @pl.when(h < early + direct)
            def _():
                arrived(qq.at[1, :, cols(h)], sem_c.at[h])

            other = soft([nt(k, qq[1, :, cols(h)])], [v])
            arrived(pack_r.at[h], sem_a.at[h])
            put_state(h, get_state(h).astype(jnp.float32) + state)
            arrived(st_r.at[h], sem_d.at[h])
            pass_on(h, *normalised(merge(other, st_r[h, 1:2], pack_r[h, :HEAD])))

        def for_own(h):
            q, k, v = own_qkv(h)
            phi_q, linear = local_linear(q, feature_map(k), v)
            linear = linear + tt(get_state(h), phi_q)
            own_sum = soft([diagonal(q, k)], [v])
            arrived(oa_r.at[h], sem_b.at[h])
            finish(h, merge(own_sum, st_r[h, 0:1], oa_r[h]), linear)

        def head(h):
            for_last(h)
            in_turn(h, for_own)

        each(early, whole, head)
        each(whole - lag, whole, for_own)
        arrived(out_ref.at[:, whole * HEAD :], sem_w.at[2 * count])


        def drain(count):
            sent(qq.at[0, :, count * HEAD : whole * HEAD], 0)
            sent(qq.at[1, :, (count + direct) * HEAD : whole * HEAD], 5)

        by_early(drain)
        sent(whole_in.at[:, 0:3], 1)
        sent(pack_s.at[0:whole], 2)
        sent(st_s.at[0:whole], 3)

    @pl.when(me == 3)
    def _():
        def to_hub(h):
            move(
                q_ref.at[:, cols(h)], qq.at[1, :, cols(h)], sem_s.at[2], sem_b.at[h], 1
            ).start()

        def to_left(h):
            move(
                q_ref.at[:, cols(h)], qq.at[1, :, cols(h)], sem_s.at[0], sem_c.at[h], 2
            ).start()

        each(early, early + direct, to_hub)
        each(early + direct, whole, to_left)
        each(0, early + direct, to_left)

        wait_loads()

        def compute(h):
            q, k, v = own_qkv(h)
            phi_q, linear = local_linear(q, feature_map(k), v)
            own_sum = soft([diagonal(q, k)], [v])
            arrived(pack_r.at[h], sem_a.at[h])
            linear = linear + tt(get_state(h), phi_q)
            arrived(st_r.at[h], sem_d.at[h])
            finish(h, merge(own_sum, st_r[h, 0:1], pack_r[h, :HEAD]), linear)

        each(0, turn, compute)
        for c in range(count):
            for i, src in enumerate((q_ref, k_ref, v_ref)):
                to_whole(c, 2 + i, src, c)
        each(turn, whole, compute)
        arrived(out_ref.at[:, whole * HEAD :], sem_w.at[2 * count])

        sent(qq.at[1, :, : whole * HEAD], 0)
        sent(whole_in.at[:, 0:3], 1)
        by_early(lambda count: sent(qq.at[1, :, count * HEAD : (count + direct) * HEAD], 2))


def hub_shards(queries, key_vectors, value_vectors, norm_gain, window_gain):
    tok, width = queries.shape
    heads = width // HEAD
    most, _, _, whole = classes(heads)
    count = heads - whole
    hbm = pl.BlockSpec(memory_space=pl.ANY)
    pack = pltpu.VMEM((heads, HEAD + HEAD * HEAD // tok, tok), jnp.bfloat16)
    partial = pltpu.VMEM((heads, HEAD, tok), jnp.bfloat16)
    stats = pltpu.VMEM((heads, 2, tok), jnp.float32)
    dma = pltpu.SemaphoreType.DMA
    return pl.pallas_call(
        hub_kernel,
        out_shape=pltpu.VMEM((tok, width), jnp.bfloat16),
        in_specs=[hbm] * 5,
        out_specs=pl.BlockSpec(memory_space=pltpu.VMEM),
        scratch_shapes=[
            pltpu.VMEM((2, tok, width), jnp.bfloat16),
            pltpu.VMEM((2, tok, width), jnp.bfloat16),
            pltpu.VMEM((3, tok, width), jnp.bfloat16),
            pltpu.VMEM((2, heads, HEAD), jnp.float32),
            pltpu.VMEM((4, most, tok, HEAD), jnp.bfloat16),
            pltpu.VMEM((count, 6, tok, HEAD), jnp.bfloat16),
            pltpu.VMEM((count, 2, tok, HEAD), jnp.bfloat16),
        ]
        + [pack] * 2
        + [partial] * 2
        + [stats] * 2
        + [dma((heads,))] * 4
        + [dma((2 * count + 1,)), dma((6,)), dma((2,))],
        compiler_params=pltpu.CompilerParams(
            collective_id=0, has_side_effects=True, vmem_limit_bytes=56 * 2**20
        ),
        name="hub_attention",
    )(
        queries,
        key_vectors,
        value_vectors,
        norm_gain.reshape(heads, HEAD),
        window_gain.reshape(heads, HEAD),
    )


def solution(mesh):
    count = mesh.shape["ctx"]

    def run(queries, key_vectors, value_vectors, norm_gain, window_gain):
        args = (queries, key_vectors, value_vectors, norm_gain, window_gain)
        fits = count * queries.shape[0] <= WINDOW
        tok, width = queries.shape
        even = tok % HEAD == 0 and HEAD * HEAD % (16 * tok) == 0
        if fits and even and count == 4 and width >= 16 * HEAD:
            return hub_shards(*args)
        return shards(*args)

    return jax.shard_map(
        run,
        mesh=mesh,
        in_specs=(P(("dp", "ctx"), None), P(("dp", "ctx"), None), P(("dp", "ctx"), None), P(), P()),
        out_specs=P(("dp", "ctx"), None),
        check_vma=False,
    )
```

```python
import functools
import math

import jax
import jax.numpy as jnp
from jax import lax
from jax.experimental import pallas as pl
from jax.experimental.pallas import tpu as pltpu
from jax.sharding import PartitionSpec as P

HEAD = 128
WINDOW = 1024
EPS = 1e-05


def passed_along(value, axis, steps):
    count = lax.axis_size(axis)
    leading, last = (max(0, -steps), min(count, count - steps))
    return lax.ppermute(value, axis, [(source, source + steps) for source in range(leading, last)])


def entering(array, axis, combine, identity):
    peers, position = (lax.axis_size(axis), lax.axis_index(axis))
    everything = lax.all_gather(array.astype(jnp.bfloat16), axis)
    start = jnp.broadcast_to(jnp.asarray(identity, array.dtype), array.shape)

    def lap(k, before):
        reached = k < position
        new = combine(before, everything[k].astype(array.dtype))
        return jnp.where(reached, new, before)

    return lax.fori_loop(0, peers, lap, start)


def feature_map(values):
    upcast = values.astype(jnp.float32)
    return jnp.where(upcast > 0, upcast + 1.0, jnp.exp(jnp.minimum(upcast, 0.0))).astype(
        jnp.bfloat16
    )


def add_states(earlier, later):
    return earlier + later


def shards(queries, key_vectors, value_vectors, norm_gain, window_gain):
    tok_rows, model_width = queries.shape
    head_count = model_width // HEAD
    ctx_index = lax.axis_index("ctx")
    reach_blocks = WINDOW // tok_rows
    own_pair = (key_vectors, value_vectors)
    received = []
    travelling = own_pair
    for distance in range(reach_blocks):
        travelling = passed_along((travelling[0], travelling[1]), "ctx", 1)
        received.append(travelling)
    ordered = received[::-1] + [own_pair]
    window_keys = jnp.concatenate([member[0] for member in ordered], axis=0)
    window_values = jnp.concatenate([member[1] for member in ordered], axis=0)
    span_rows = window_keys.shape[0]
    query_place = ctx_index * tok_rows + jnp.arange(tok_rows, dtype=jnp.int32)
    key_place = (ctx_index - reach_blocks) * tok_rows + jnp.arange(span_rows, dtype=jnp.int32)
    inside = (
        (key_place[None, :] <= query_place[:, None])
        & (query_place[:, None] - key_place[None, :] < WINDOW)
        & (key_place[None, :] >= 0)
    )
    group_size = 4
    groups = head_count // group_size
    scale = 1.0 / math.sqrt(HEAD)

    def split_groups(matrix):
        return jnp.moveaxis(matrix.reshape(matrix.shape[0], groups, group_size, HEAD), 1, 0)

    def attend(operands):
        query_group, key_group, value_group = operands
        scores = (
            jnp.einsum("tge,sge->gts", query_group, key_group, preferred_element_type=jnp.float32)
            * scale
        )
        scores = jnp.where(inside[None], scores, -jnp.inf)
        peak = jnp.max(scores, axis=-1, keepdims=True)
        expos = jnp.exp(scores - peak)
        weights = (expos / jnp.sum(expos, axis=-1, keepdims=True)).astype(jnp.bfloat16)
        return jnp.einsum("gts,sge->tge", weights, value_group, preferred_element_type=jnp.float32)

    attended = lax.map(
        attend, (split_groups(queries), split_groups(window_keys), split_groups(window_values))
    )
    attended = jnp.moveaxis(attended, 0, 1).reshape(tok_rows, head_count, HEAD)
    windowed = attended * lax.rsqrt(jnp.mean(attended * attended, axis=-1, keepdims=True) + EPS)
    windowed = windowed * window_gain.reshape(head_count, HEAD)
    phi_query = feature_map(queries).reshape(tok_rows, head_count, HEAD)
    phi_key = feature_map(key_vectors).reshape(tok_rows, head_count, HEAD)
    value_heads = value_vectors.reshape(tok_rows, head_count, HEAD)
    local_state = jnp.einsum(
        "the,thf->hef", phi_key, value_heads, preferred_element_type=jnp.float32
    )
    carried = entering(local_state, "ctx", add_states, jnp.zeros_like(local_state))
    from_state = jnp.einsum(
        "the,hef->thf", phi_query, carried.astype(jnp.bfloat16), preferred_element_type=jnp.float32
    )
    affinity = jnp.einsum("the,she->hts", phi_query, phi_key, preferred_element_type=jnp.float32)
    inner = jnp.arange(tok_rows, dtype=jnp.int32)
    causal = inner[:, None] >= inner[None, :]
    affinity = jnp.where(causal[None], affinity, 0.0).astype(jnp.bfloat16)
    local_part = jnp.einsum(
        "hts,shf->thf", affinity, value_heads, preferred_element_type=jnp.float32
    )
    linear = from_state + local_part
    normed = linear * lax.rsqrt(jnp.mean(linear * linear, axis=-1, keepdims=True) + EPS)
    normed = normed * norm_gain.reshape(head_count, HEAD)
    return (windowed + normed).reshape(tok_rows, model_width).astype(jnp.bfloat16)


EXP_SCALE = math.log2(math.e) / math.sqrt(HEAD)
LOW = -1e30


def nt(a, b):
    return lax.dot_general(a, b, (((1,), (1,)), ((), ())), preferred_element_type=jnp.float32)


def tn(a, b):
    return lax.dot_general(a, b, (((0,), (0,)), ((), ())), preferred_element_type=jnp.float32)


def tt(a, b):
    return lax.dot_general(a, b, (((0,), (1,)), ((), ())), preferred_element_type=jnp.float32)


DIRECT = 2


def classes(heads):
    return heads // 8, heads // 16, heads // 2, heads - heads // 8


def hub_kernel(
    q_ref, k_ref, v_ref, gn_ref, gw_ref, out_ref,
    kv0, qq, own, gains, early_kv, whole_in, whole_out, pack_s, pack_r, oa_s, oa_r, st_s, st_r,
    tally, sem_a, sem_b, sem_w, sem_s, loaded,
):
    tok, width = q_ref.shape
    heads = width // HEAD
    most, least, cut, whole = classes(heads)
    count = heads - whole
    depth = HEAD * HEAD // tok
    me = lax.axis_index("ctx")
    fewer = lax.rem(lax.axis_index("dp"), 2)
    early = most + fewer * (least - most)
    spare = 2 * count + 1
    turn = 7
    lag = 2
    MESH = pl.DeviceIdType.MESH

    def cols(h):
        if isinstance(h, int):
            return pl.ds(h * HEAD, HEAD)
        return pl.ds(pl.multiple_of(h * HEAD, HEAD), HEAD)

    def move(src, dst, sent, arrived, target):
        return pltpu.make_async_remote_copy(
            src_ref=src,
            dst_ref=dst,
            send_sem=sent,
            recv_sem=arrived,
            device_id={"ctx": target},
            device_id_type=MESH,
        )

    def arrived(ref, sem):
        move(ref, ref, sem_s.at[0], sem, 0).wait_recv()

    def sent(ref, i):
        move(ref, ref, sem_s.at[i], sem_w.at[0], 0).wait_send()

    def to_whole(c, i, src, sem):
        move(
            src.at[:, cols(whole + c)], whole_in.at[c, i], sem_s.at[1], sem_w.at[sem], 1
        ).start()

    def each(start, stop, body):
        def step(h, carry):
            body(h)
            return carry

        lax.fori_loop(start, stop, step, 0)

    def by_early(body):
        for which, count in enumerate((most, least)):

            @pl.when(fewer == which)
            def _():
                body(count)

    skips = [cut + 2 * i for i in range(lag)]

    def in_turn(h, body):
        late = sum((h >= at).astype(jnp.int32) for at in skips)

        @pl.when(functools.reduce(jnp.logical_and, [h != at for at in skips]))
        def _():
            body(h - late)

    loads = [
        pltpu.make_async_copy(src, own.at[i], loaded.at[0])
        for i, src in enumerate([q_ref, k_ref, v_ref])
    ] + [
        pltpu.make_async_copy(src, gains.at[i], loaded.at[1])
        for i, src in enumerate([gn_ref, gw_ref])
    ]
    for load in loads:
        load.start()

    def wait_loads():
        pltpu.make_async_copy(own, own, loaded.at[0]).wait()
        pltpu.make_async_copy(gains, gains, loaded.at[1]).wait()

    barrier = pltpu.get_barrier_semaphore()
    senders = {1: (0, 2, 3), 2: (1, 3)}
    for device, others in senders.items():

        @pl.when(me == device)
        def _():
            for other in others:
                pl.semaphore_signal(
                    barrier, inc=1, device_id={"ctx": other}, device_id_type=MESH
                )

    pl.semaphore_wait(barrier, 1 + (me == 3).astype(jnp.int32))

    key_at = lax.broadcasted_iota(jnp.int32, (tok, tok), 0)
    query_at = lax.broadcasted_iota(jnp.int32, (tok, tok), 1)
    causal = key_at <= query_at

    def own_qkv(h):
        return own[0, :, cols(h)], own[1, :, cols(h)], own[2, :, cols(h)]

    def soft(scores, values):
        peak = functools.reduce(
            jnp.maximum, [jnp.max(s, axis=0, keepdims=True) for s in scores]
        )
        total, out = 0.0, 0.0
        for s, v in zip(scores, values):
            e = jnp.exp2((s - peak) * EXP_SCALE)
            total = total + jnp.sum(e, axis=0, keepdims=True)
            out = out + tn(v, e.astype(jnp.bfloat16))
        return peak, total, out

    def normalised(soft_sum):
        peak, total, out = soft_sum
        return peak + jnp.log2(total) * (1.0 / EXP_SCALE), out * (1.0 / total)

    def merge(one, level, out):
        top = jnp.maximum(one[0], level)
        f1 = jnp.exp2((one[0] - top) * EXP_SCALE)
        f2 = jnp.exp2((level - top) * EXP_SCALE)
        return top, one[1] * f1 + f2, one[2] * f1 + out.astype(jnp.float32) * f2

    def local_linear(q, phi_k, v):
        phi_q = feature_map(q)
        affinity = jnp.where(causal, nt(phi_k, phi_q), 0.0).astype(jnp.bfloat16)
        return phi_q, tn(v, affinity)

    def rows_of(h, soft_sum, linear):
        _, total, out = soft_sum
        att = out * (1.0 / total)
        att = att * lax.rsqrt(jnp.mean(att * att, axis=0, keepdims=True) + EPS)
        lin = linear * lax.rsqrt(jnp.mean(linear * linear, axis=0, keepdims=True) + EPS)
        row = att.T * gains[1, pl.ds(h, 1), :] + lin.T * gains[0, pl.ds(h, 1), :]
        return row.astype(jnp.bfloat16)

    def finish(h, soft_sum, linear):
        out_ref[:, cols(h)] = rows_of(h, soft_sum, linear)

    def diagonal(q, k):
        return jnp.where(causal, nt(k, q), LOW)

    def put_state(h, state):
        for i in range(tok // HEAD):
            pack_s[h, HEAD : HEAD + depth, i * HEAD : (i + 1) * HEAD] = state[
                i * depth : (i + 1) * depth
            ].astype(jnp.bfloat16)

    def get_state(h):
        pieces = [
            pack_r[h, HEAD : HEAD + depth, i * HEAD : (i + 1) * HEAD] for i in range(tok // HEAD)
        ]
        return jnp.concatenate(pieces, axis=0)

    def pack_right(h, i, target):
        move(pack_s.at[h], pack_r.at[h], sem_s.at[i], sem_a.at[h], target).start()

    def st_right(h, i, target):
        move(st_s.at[h], st_r.at[h], sem_s.at[i], sem_a.at[h], target).start()

    def pack_arrived(h):
        arrived(tally, sem_a.at[h])

    @pl.when(me == 0)
    def _():
        def start(h):
            for i, src in enumerate((k_ref, v_ref)):
                move(
                    src.at[:, cols(h)], kv0.at[i, :, cols(h)], sem_s.at[0], sem_a.at[h], 1
                ).start()

        each(0, heads, start)

        wait_loads()

        def compute(h):
            q, k, v = own_qkv(h)
            _, linear = local_linear(q, feature_map(k), v)
            finish(h, soft([diagonal(q, k)], [v]), linear)

        each(0, heads, compute)
        sent(kv0, 0)

    @pl.when(me == 1)
    def _():
        def to_early(i, src, h):
            move(src, early_kv.at[i, h], sem_s.at[0], sem_a.at[h], 2).start()

        def start(h):
            to_early(2, k_ref.at[:, cols(h)], h)
            to_early(3, v_ref.at[:, cols(h)], h)

        each(0, early, start)

        wait_loads()

        def own_rows(h, q, k, v, k0, v0, phi_k, before):
            phi_q, linear = local_linear(q, phi_k, v)
            linear = linear + tt(before.astype(jnp.bfloat16), phi_q)
            finish(h, soft([nt(k0, q), diagonal(q, k)], [v0, v]), linear)

        def early_head(h):
            q, k, v = own_qkv(h)
            arrived(kv0.at[:, :, cols(h)], sem_a.at[h])
            to_early(0, kv0.at[0, :, cols(h)], h)
            to_early(1, kv0.at[1, :, cols(h)], h)
            k0, v0 = kv0[0, :, cols(h)], kv0[1, :, cols(h)]
            before = tn(feature_map(k0), v0)
            own_rows(h, q, k, v, k0, v0, feature_map(k), before)

        each(0, early, early_head)

        def oa_right(h):
            move(oa_s.at[h], oa_r.at[h], sem_s.at[3], sem_b.at[h], 2).start()

        def shared_head(h):
            q, k, v = own_qkv(h)
            phi_k = feature_map(k)
            state = tn(phi_k, v)
            arrived(kv0.at[:, :, cols(h)], sem_a.at[h])
            k0, v0 = kv0[0, :, cols(h)], kv0[1, :, cols(h)]
            before = tn(feature_map(k0), v0)
            put_state(h, before + state)
            arrived(qq.at[:, :, cols(h)], sem_b.at[h])

            def part(i):
                other = qq[i, :, cols(h)]
                level, out = normalised(soft([nt(k0, other), nt(k, other)], [v0, v]))
                st_s[h, i : i + 1] = level
                return out.astype(jnp.bfloat16)

            pack_s[h, :HEAD] = part(1)
            pack_right(h, 1, 2)
            oa_s[h] = part(0)
            st_right(h, 2, 2)

            in_turn(h, oa_right)
            own_rows(h, q, k, v, k0, v0, phi_k, before)

        def out_right(c, i, target):
            move(
                whole_out.at[c, i],
                out_ref.at[:, cols(whole + c)],
                sem_s.at[4],
                sem_w.at[2 * count],
                target,
            ).start()

        def whole_head(c):
            h = whole + c
            q, k, v = own_qkv(h)
            phi_k = feature_map(k)
            arrived(kv0.at[:, :, cols(h)], sem_a.at[h])
            k0, v0 = kv0[0, :, cols(h)], kv0[1, :, cols(h)]
            before = tn(feature_map(k0), v0)
            own_rows(h, q, k, v, k0, v0, phi_k, before)
            before = before + tn(phi_k, v)
            arrived(whole_in.at[c, 0:5], sem_w.at[c])
            k2, v2, q3, k3, v3 = [whole_in[c, i] for i in range(5)]
            phi_k2 = feature_map(k2)
            after = before + tn(phi_k2, v2)
            phi_q, linear = local_linear(q3, feature_map(k3), v3)
            linear = linear + tt(after.astype(jnp.bfloat16), phi_q)
            scores = [nt(k0, q3), nt(k, q3), nt(k2, q3), diagonal(q3, k3)]
            whole_out[c, 1] = rows_of(h, soft(scores, [v0, v, v2, v3]), linear)
            out_right(c, 1, 3)
            arrived(whole_in.at[c, 5], sem_w.at[count + c])
            q2 = whole_in[c, 5]
            phi_q, linear = local_linear(q2, phi_k2, v2)
            linear = linear + tt(before.astype(jnp.bfloat16), phi_q)
            scores = [nt(k0, q2), nt(k, q2), diagonal(q2, k2)]
            whole_out[c, 0] = rows_of(h, soft(scores, [v0, v, v2]), linear)
            out_right(c, 0, 2)

        each(early, whole, shared_head)
        each(whole - lag, whole, oa_right)
        each(0, count, whole_head)

        def drain(count):
            sent(early_kv.at[:, 0:count], 0)
            sent(pack_s.at[count:whole], 1)
            sent(st_s.at[count:whole], 2)
            sent(oa_s.at[count:whole], 3)

        by_early(drain)
        sent(whole_out, 4)

    @pl.when(me == 2)
    def _():
        def start(h):
            move(
                q_ref.at[:, cols(h)], qq.at[0, :, cols(h)], sem_s.at[0], sem_b.at[h], 1
            ).start()

        def relay(h):
            start(h)
            q3 = qq.at[1, :, cols(h)]
            arrived(q3, sem_b.at[h])
            move(q3, q3, sem_s.at[5], sem_b.at[h], 1).start()

        each(early, early + DIRECT, start)
        each(early + DIRECT, whole, relay)
        for c in range(count):
            for i, src, sem in ((0, k_ref, c), (1, v_ref, c), (5, q_ref, count + c)):
                to_whole(c, i, src, sem)

        wait_loads()

        def pass_on(h, level, out):
            pack_s[h, :HEAD] = out.astype(jnp.bfloat16)
            st_s[h, 0:1] = level
            st_s[h, 1:2] = level
            pack_right(h, 2, 3)
            st_right(h, 3, 3)

        def early_head(h):
            q, k, v = own_qkv(h)
            arrived(early_kv.at[:, h], sem_a.at[h])
            arrived(qq.at[1, :, cols(h)], sem_b.at[h])
            k0, v0, k1, v1 = [early_kv[i, h] for i in range(4)]
            phi_k = feature_map(k)
            before = tn(feature_map(k0), v0) + tn(feature_map(k1), v1)
            put_state(h, before + tn(phi_k, v))
            q3 = qq[1, :, cols(h)]
            other = soft([nt(k0, q3), nt(k1, q3), nt(k, q3)], [v0, v1, v])
            pass_on(h, *normalised(other))
            phi_q, linear = local_linear(q, phi_k, v)
            linear = linear + tt(before.astype(jnp.bfloat16), phi_q)
            scores = [nt(k0, q), nt(k1, q), diagonal(q, k)]
            finish(h, soft(scores, [v0, v1, v]), linear)

        each(0, early, early_head)

        def for_last(h):
            k, v = own[1, :, cols(h)], own[2, :, cols(h)]
            state = tn(feature_map(k), v)

            @pl.when(h < early + DIRECT)
            def _():
                arrived(qq.at[1, :, cols(h)], sem_w.at[spare + h - early])

            other = soft([nt(k, qq[1, :, cols(h)])], [v])
            pack_arrived(h)
            put_state(h, get_state(h).astype(jnp.float32) + state)
            pass_on(h, *normalised(merge(other, st_r[h, 1:2], pack_r[h, :HEAD])))

        def for_own(h):
            q, k, v = own_qkv(h)
            phi_q, linear = local_linear(q, feature_map(k), v)
            linear = linear + tt(get_state(h), phi_q)
            own_sum = soft([diagonal(q, k)], [v])
            arrived(oa_r.at[h], sem_b.at[h])
            finish(h, merge(own_sum, st_r[h, 0:1], oa_r[h]), linear)

        def head(h):
            for_last(h)
            in_turn(h, for_own)

        each(early, whole, head)
        each(whole - lag, whole, for_own)
        arrived(out_ref.at[:, whole * HEAD :], sem_w.at[2 * count])


        def drain(count):
            sent(qq.at[0, :, count * HEAD : whole * HEAD], 0)
            sent(qq.at[1, :, (count + DIRECT) * HEAD : whole * HEAD], 5)

        by_early(drain)
        sent(whole_in.at[:, 0:3], 1)
        sent(pack_s.at[0:whole], 2)
        sent(st_s.at[0:whole], 3)

    @pl.when(me == 3)
    def _():
        def to_hub(h):
            move(
                q_ref.at[:, cols(h)], qq.at[1, :, cols(h)], sem_s.at[2], sem_b.at[h], 1
            ).start()

        def to_left(h, sem):
            move(q_ref.at[:, cols(h)], qq.at[1, :, cols(h)], sem_s.at[0], sem, 2).start()

        each(early, early + DIRECT, to_hub)
        each(early + DIRECT, whole, lambda h: to_left(h, sem_b.at[h]))
        each(0, early, lambda h: to_left(h, sem_b.at[h]))
        each(0, DIRECT, lambda i: to_left(early + i, sem_w.at[spare + i]))

        wait_loads()

        def compute(h):
            q, k, v = own_qkv(h)
            phi_q, linear = local_linear(q, feature_map(k), v)
            own_sum = soft([diagonal(q, k)], [v])
            pack_arrived(h)
            linear = linear + tt(get_state(h), phi_q)
            finish(h, merge(own_sum, st_r[h, 0:1], pack_r[h, :HEAD]), linear)

        each(0, turn, compute)
        for c in range(count):
            for i, src in enumerate((q_ref, k_ref, v_ref)):
                to_whole(c, 2 + i, src, c)
        each(turn, whole, compute)
        arrived(out_ref.at[:, whole * HEAD :], sem_w.at[2 * count])

        sent(qq.at[1, :, : whole * HEAD], 0)
        sent(whole_in.at[:, 0:3], 1)
        by_early(lambda count: sent(qq.at[1, :, count * HEAD : (count + DIRECT) * HEAD], 2))


def hub_shards(queries, key_vectors, value_vectors, norm_gain, window_gain):
    tok, width = queries.shape
    heads = width // HEAD
    most, _, _, whole = classes(heads)
    count = heads - whole
    hbm = pl.BlockSpec(memory_space=pl.ANY)
    pack = pltpu.VMEM((heads, HEAD + HEAD * HEAD // tok, tok), jnp.bfloat16)
    partial = pltpu.VMEM((heads, HEAD, tok), jnp.bfloat16)
    stats = pltpu.VMEM((heads, 2, tok), jnp.float32)
    dma = pltpu.SemaphoreType.DMA
    return pl.pallas_call(
        hub_kernel,
        out_shape=pltpu.VMEM((tok, width), jnp.bfloat16),
        in_specs=[hbm] * 5,
        out_specs=pl.BlockSpec(memory_space=pltpu.VMEM),
        scratch_shapes=[
            pltpu.VMEM((2, tok, width), jnp.bfloat16),
            pltpu.VMEM((2, tok, width), jnp.bfloat16),
            pltpu.VMEM((3, tok, width), jnp.bfloat16),
            pltpu.VMEM((2, heads, HEAD), jnp.float32),
            pltpu.VMEM((4, most, tok, HEAD), jnp.bfloat16),
            pltpu.VMEM((count, 6, tok, HEAD), jnp.bfloat16),
            pltpu.VMEM((count, 2, tok, HEAD), jnp.bfloat16),
        ]
        + [pack] * 2
        + [partial] * 2
        + [stats] * 2
        + [pltpu.VMEM(((HEAD + HEAD * HEAD // tok) // 4 + 1, 2, tok), jnp.float32)]
        + [dma((heads,))] * 2
        + [dma((2 * count + 1 + DIRECT,)), dma((6,)), dma((2,))],
        compiler_params=pltpu.CompilerParams(
            collective_id=0, has_side_effects=True, vmem_limit_bytes=56 * 2**20
        ),
        name="hub_attention",
    )(
        queries,
        key_vectors,
        value_vectors,
        norm_gain.reshape(heads, HEAD),
        window_gain.reshape(heads, HEAD),
    )


def solution(mesh):
    count = mesh.shape["ctx"]

    def run(queries, key_vectors, value_vectors, norm_gain, window_gain):
        args = (queries, key_vectors, value_vectors, norm_gain, window_gain)
        fits = count * queries.shape[0] <= WINDOW
        tok, width = queries.shape
        even = tok % HEAD == 0 and HEAD * HEAD % (16 * tok) == 0
        if fits and even and count == 4 and width >= 16 * HEAD:
            return hub_shards(*args)
        return shards(*args)

    return jax.shard_map(
        run,
        mesh=mesh,
        in_specs=(P(("dp", "ctx"), None), P(("dp", "ctx"), None), P(("dp", "ctx"), None), P(), P()),
        out_specs=P(("dp", "ctx"), None),
        check_vma=False,
    )
```

```python
import functools
import math

import jax
import jax.numpy as jnp
from jax import lax
from jax.experimental import pallas as pl
from jax.experimental.pallas import tpu as pltpu
from jax.sharding import PartitionSpec as P

HEAD = 128
WINDOW = 1024
EPS = 1e-05


def passed_along(value, axis, steps):
    count = lax.axis_size(axis)
    leading, last = (max(0, -steps), min(count, count - steps))
    return lax.ppermute(value, axis, [(source, source + steps) for source in range(leading, last)])


def entering(array, axis, combine, identity):
    peers, position = (lax.axis_size(axis), lax.axis_index(axis))
    everything = lax.all_gather(array.astype(jnp.bfloat16), axis)
    start = jnp.broadcast_to(jnp.asarray(identity, array.dtype), array.shape)

    def lap(k, before):
        reached = k < position
        new = combine(before, everything[k].astype(array.dtype))
        return jnp.where(reached, new, before)

    return lax.fori_loop(0, peers, lap, start)


def feature_map(values):
    upcast = values.astype(jnp.float32)
    return jnp.where(upcast > 0, upcast + 1.0, jnp.exp(jnp.minimum(upcast, 0.0))).astype(
        jnp.bfloat16
    )


def add_states(earlier, later):
    return earlier + later


def shards(queries, key_vectors, value_vectors, norm_gain, window_gain):
    tok_rows, model_width = queries.shape
    head_count = model_width // HEAD
    ctx_index = lax.axis_index("ctx")
    reach_blocks = WINDOW // tok_rows
    own_pair = (key_vectors, value_vectors)
    received = []
    travelling = own_pair
    for distance in range(reach_blocks):
        travelling = passed_along((travelling[0], travelling[1]), "ctx", 1)
        received.append(travelling)
    ordered = received[::-1] + [own_pair]
    window_keys = jnp.concatenate([member[0] for member in ordered], axis=0)
    window_values = jnp.concatenate([member[1] for member in ordered], axis=0)
    span_rows = window_keys.shape[0]
    query_place = ctx_index * tok_rows + jnp.arange(tok_rows, dtype=jnp.int32)
    key_place = (ctx_index - reach_blocks) * tok_rows + jnp.arange(span_rows, dtype=jnp.int32)
    inside = (
        (key_place[None, :] <= query_place[:, None])
        & (query_place[:, None] - key_place[None, :] < WINDOW)
        & (key_place[None, :] >= 0)
    )
    group_size = 4
    groups = head_count // group_size
    scale = 1.0 / math.sqrt(HEAD)

    def split_groups(matrix):
        return jnp.moveaxis(matrix.reshape(matrix.shape[0], groups, group_size, HEAD), 1, 0)

    def attend(operands):
        query_group, key_group, value_group = operands
        scores = (
            jnp.einsum("tge,sge->gts", query_group, key_group, preferred_element_type=jnp.float32)
            * scale
        )
        scores = jnp.where(inside[None], scores, -jnp.inf)
        peak = jnp.max(scores, axis=-1, keepdims=True)
        expos = jnp.exp(scores - peak)
        weights = (expos / jnp.sum(expos, axis=-1, keepdims=True)).astype(jnp.bfloat16)
        return jnp.einsum("gts,sge->tge", weights, value_group, preferred_element_type=jnp.float32)

    attended = lax.map(
        attend, (split_groups(queries), split_groups(window_keys), split_groups(window_values))
    )
    attended = jnp.moveaxis(attended, 0, 1).reshape(tok_rows, head_count, HEAD)
    windowed = attended * lax.rsqrt(jnp.mean(attended * attended, axis=-1, keepdims=True) + EPS)
    windowed = windowed * window_gain.reshape(head_count, HEAD)
    phi_query = feature_map(queries).reshape(tok_rows, head_count, HEAD)
    phi_key = feature_map(key_vectors).reshape(tok_rows, head_count, HEAD)
    value_heads = value_vectors.reshape(tok_rows, head_count, HEAD)
    local_state = jnp.einsum(
        "the,thf->hef", phi_key, value_heads, preferred_element_type=jnp.float32
    )
    carried = entering(local_state, "ctx", add_states, jnp.zeros_like(local_state))
    from_state = jnp.einsum(
        "the,hef->thf", phi_query, carried.astype(jnp.bfloat16), preferred_element_type=jnp.float32
    )
    affinity = jnp.einsum("the,she->hts", phi_query, phi_key, preferred_element_type=jnp.float32)
    inner = jnp.arange(tok_rows, dtype=jnp.int32)
    causal = inner[:, None] >= inner[None, :]
    affinity = jnp.where(causal[None], affinity, 0.0).astype(jnp.bfloat16)
    local_part = jnp.einsum(
        "hts,shf->thf", affinity, value_heads, preferred_element_type=jnp.float32
    )
    linear = from_state + local_part
    normed = linear * lax.rsqrt(jnp.mean(linear * linear, axis=-1, keepdims=True) + EPS)
    normed = normed * norm_gain.reshape(head_count, HEAD)
    return (windowed + normed).reshape(tok_rows, model_width).astype(jnp.bfloat16)


EXP_SCALE = math.log2(math.e) / math.sqrt(HEAD)
LOW = -1e30


def nt(a, b):
    return lax.dot_general(a, b, (((1,), (1,)), ((), ())), preferred_element_type=jnp.float32)


def tn(a, b):
    return lax.dot_general(a, b, (((0,), (0,)), ((), ())), preferred_element_type=jnp.float32)


def tt(a, b):
    return lax.dot_general(a, b, (((0,), (1,)), ((), ())), preferred_element_type=jnp.float32)


DIRECT = 3


def classes(heads):
    return heads // 8, heads // 16, heads // 2, heads - heads // 8


def hub_kernel(
    q_ref, k_ref, v_ref, gn_ref, gw_ref, out_ref,
    kv0, qq, own, gains, early_kv, whole_in, whole_out, pack_s, pack_r, oa_s, oa_r, st_s, st_r,
    tally, sem_a, sem_b, sem_w, sem_s, loaded,
):
    tok, width = q_ref.shape
    heads = width // HEAD
    most, least, cut, whole = classes(heads)
    count = heads - whole
    depth = HEAD * HEAD // tok
    me = lax.axis_index("ctx")
    fewer = lax.rem(lax.axis_index("dp"), 2)
    early = most + fewer * (least - most)
    spare = 2 * count + 1
    turn = 7
    lag = 2
    MESH = pl.DeviceIdType.MESH

    def cols(h):
        if isinstance(h, int):
            return pl.ds(h * HEAD, HEAD)
        return pl.ds(pl.multiple_of(h * HEAD, HEAD), HEAD)

    def move(src, dst, sent, arrived, target):
        return pltpu.make_async_remote_copy(
            src_ref=src,
            dst_ref=dst,
            send_sem=sent,
            recv_sem=arrived,
            device_id={"ctx": target},
            device_id_type=MESH,
        )

    def arrived(ref, sem):
        move(ref, ref, sem_s.at[0], sem, 0).wait_recv()

    def sent(ref, i):
        move(ref, ref, sem_s.at[i], sem_w.at[0], 0).wait_send()

    def to_whole(c, i, src, sem):
        move(
            src.at[:, cols(whole + c)], whole_in.at[c, i], sem_s.at[1], sem_w.at[sem], 1
        ).start()

    def each(start, stop, body):
        def step(h, carry):
            body(h)
            return carry

        lax.fori_loop(start, stop, step, 0)

    def by_early(body):
        for which, count in enumerate((most, least)):

            @pl.when(fewer == which)
            def _():
                body(count)

    skips = [cut + 2 * i for i in range(lag)]

    def in_turn(h, body):
        late = sum((h >= at).astype(jnp.int32) for at in skips)

        @pl.when(functools.reduce(jnp.logical_and, [h != at for at in skips]))
        def _():
            body(h - late)

    loads = [
        pltpu.make_async_copy(src, own.at[i], loaded.at[0])
        for i, src in enumerate([q_ref, k_ref, v_ref])
    ] + [
        pltpu.make_async_copy(src, gains.at[i], loaded.at[1])
        for i, src in enumerate([gn_ref, gw_ref])
    ]
    for load in loads:
        load.start()

    def wait_loads():
        pltpu.make_async_copy(own, own, loaded.at[0]).wait()
        pltpu.make_async_copy(gains, gains, loaded.at[1]).wait()

    barrier = pltpu.get_barrier_semaphore()
    senders = {1: (0, 2, 3), 2: (1, 3)}
    for device, others in senders.items():

        @pl.when(me == device)
        def _():
            for other in others:
                pl.semaphore_signal(
                    barrier, inc=1, device_id={"ctx": other}, device_id_type=MESH
                )

    pl.semaphore_wait(barrier, 1 + (me == 3).astype(jnp.int32))

    key_at = lax.broadcasted_iota(jnp.int32, (tok, tok), 0)
    query_at = lax.broadcasted_iota(jnp.int32, (tok, tok), 1)
    causal = key_at <= query_at

    def own_qkv(h):
        return own[0, :, cols(h)], own[1, :, cols(h)], own[2, :, cols(h)]

    def soft(scores, values):
        peak = functools.reduce(
            jnp.maximum, [jnp.max(s, axis=0, keepdims=True) for s in scores]
        )
        total, out = 0.0, 0.0
        for s, v in zip(scores, values):
            e = jnp.exp2((s - peak) * EXP_SCALE)
            total = total + jnp.sum(e, axis=0, keepdims=True)
            out = out + tn(v, e.astype(jnp.bfloat16))
        return peak, total, out

    def normalised(soft_sum):
        peak, total, out = soft_sum
        return peak + jnp.log2(total) * (1.0 / EXP_SCALE), out * (1.0 / total)

    def merge(one, level, out):
        top = jnp.maximum(one[0], level)
        f1 = jnp.exp2((one[0] - top) * EXP_SCALE)
        f2 = jnp.exp2((level - top) * EXP_SCALE)
        return top, one[1] * f1 + f2, one[2] * f1 + out.astype(jnp.float32) * f2

    def local_linear(q, phi_k, v):
        phi_q = feature_map(q)
        affinity = jnp.where(causal, nt(phi_k, phi_q), 0.0).astype(jnp.bfloat16)
        return phi_q, tn(v, affinity)

    def rows_of(h, soft_sum, linear):
        _, total, out = soft_sum
        att = out * (1.0 / total)
        att = att * lax.rsqrt(jnp.mean(att * att, axis=0, keepdims=True) + EPS)
        lin = linear * lax.rsqrt(jnp.mean(linear * linear, axis=0, keepdims=True) + EPS)
        row = att.T * gains[1, pl.ds(h, 1), :] + lin.T * gains[0, pl.ds(h, 1), :]
        return row.astype(jnp.bfloat16)

    def finish(h, soft_sum, linear):
        out_ref[:, cols(h)] = rows_of(h, soft_sum, linear)

    def diagonal(q, k):
        return jnp.where(causal, nt(k, q), LOW)

    def put_state(h, state):
        for i in range(tok // HEAD):
            pack_s[h, HEAD : HEAD + depth, i * HEAD : (i + 1) * HEAD] = state[
                i * depth : (i + 1) * depth
            ].astype(jnp.bfloat16)

    def get_state(h):
        pieces = [
            pack_r[h, HEAD : HEAD + depth, i * HEAD : (i + 1) * HEAD] for i in range(tok // HEAD)
        ]
        return jnp.concatenate(pieces, axis=0)

    def pack_right(h, i, target):
        move(pack_s.at[h], pack_r.at[h], sem_s.at[i], sem_a.at[h], target).start()

    def st_right(h, i, target):
        move(st_s.at[h], st_r.at[h], sem_s.at[i], sem_a.at[h], target).start()

    def pack_arrived(h):
        arrived(tally, sem_a.at[h])

    @pl.when(me == 0)
    def _():
        def start(h):
            for i, src in enumerate((k_ref, v_ref)):
                move(
                    src.at[:, cols(h)], kv0.at[i, :, cols(h)], sem_s.at[0], sem_a.at[h], 1
                ).start()

        each(0, heads, start)

        wait_loads()

        def compute(h):
            q, k, v = own_qkv(h)
            _, linear = local_linear(q, feature_map(k), v)
            finish(h, soft([diagonal(q, k)], [v]), linear)

        each(0, heads, compute)
        sent(kv0, 0)

    @pl.when(me == 1)
    def _():
        def to_early(i, src, h):
            move(src, early_kv.at[i, h], sem_s.at[0], sem_a.at[h], 2).start()

        def start(h):
            to_early(2, k_ref.at[:, cols(h)], h)
            to_early(3, v_ref.at[:, cols(h)], h)

        each(0, early, start)

        wait_loads()

        def own_rows(h, q, k, v, k0, v0, phi_k, before):
            phi_q, linear = local_linear(q, phi_k, v)
            linear = linear + tt(before.astype(jnp.bfloat16), phi_q)
            finish(h, soft([nt(k0, q), diagonal(q, k)], [v0, v]), linear)

        def early_head(h):
            q, k, v = own_qkv(h)
            arrived(kv0.at[:, :, cols(h)], sem_a.at[h])
            to_early(0, kv0.at[0, :, cols(h)], h)
            to_early(1, kv0.at[1, :, cols(h)], h)
            k0, v0 = kv0[0, :, cols(h)], kv0[1, :, cols(h)]
            before = tn(feature_map(k0), v0)
            own_rows(h, q, k, v, k0, v0, feature_map(k), before)

        each(0, early, early_head)

        def oa_right(h):
            move(oa_s.at[h], oa_r.at[h], sem_s.at[3], sem_b.at[h], 2).start()

        def shared_head(h):
            q, k, v = own_qkv(h)
            phi_k = feature_map(k)
            state = tn(phi_k, v)
            arrived(kv0.at[:, :, cols(h)], sem_a.at[h])
            k0, v0 = kv0[0, :, cols(h)], kv0[1, :, cols(h)]
            before = tn(feature_map(k0), v0)
            put_state(h, before + state)
            arrived(qq.at[:, :, cols(h)], sem_b.at[h])

            def part(i):
                other = qq[i, :, cols(h)]
                level, out = normalised(soft([nt(k0, other), nt(k, other)], [v0, v]))
                st_s[h, i : i + 1] = level
                return out.astype(jnp.bfloat16)

            pack_s[h, :HEAD] = part(1)
            pack_right(h, 1, 2)
            oa_s[h] = part(0)
            st_right(h, 2, 2)

            in_turn(h, oa_right)
            own_rows(h, q, k, v, k0, v0, phi_k, before)

        def out_right(c, i, target):
            move(
                whole_out.at[c, i],
                out_ref.at[:, cols(whole + c)],
                sem_s.at[4],
                sem_w.at[2 * count],
                target,
            ).start()

        def whole_head(c):
            h = whole + c
            q, k, v = own_qkv(h)
            phi_k = feature_map(k)
            arrived(kv0.at[:, :, cols(h)], sem_a.at[h])
            k0, v0 = kv0[0, :, cols(h)], kv0[1, :, cols(h)]
            before = tn(feature_map(k0), v0)
            own_rows(h, q, k, v, k0, v0, phi_k, before)
            before = before + tn(phi_k, v)
            arrived(whole_in.at[c, 0:5], sem_w.at[c])
            k2, v2, q3, k3, v3 = [whole_in[c, i] for i in range(5)]
            phi_k2 = feature_map(k2)
            after = before + tn(phi_k2, v2)
            phi_q, linear = local_linear(q3, feature_map(k3), v3)
            linear = linear + tt(after.astype(jnp.bfloat16), phi_q)
            scores = [nt(k0, q3), nt(k, q3), nt(k2, q3), diagonal(q3, k3)]
            whole_out[c, 1] = rows_of(h, soft(scores, [v0, v, v2, v3]), linear)
            out_right(c, 1, 3)
            arrived(whole_in.at[c, 5], sem_w.at[count + c])
            q2 = whole_in[c, 5]
            phi_q, linear = local_linear(q2, phi_k2, v2)
            linear = linear + tt(before.astype(jnp.bfloat16), phi_q)
            scores = [nt(k0, q2), nt(k, q2), diagonal(q2, k2)]
            whole_out[c, 0] = rows_of(h, soft(scores, [v0, v, v2]), linear)
            out_right(c, 0, 2)

        each(early, whole, shared_head)
        each(whole - lag, whole, oa_right)
        each(0, count, whole_head)

        def drain(count):
            sent(early_kv.at[:, 0:count], 0)
            sent(pack_s.at[count:whole], 1)
            sent(st_s.at[count:whole], 2)
            sent(oa_s.at[count:whole], 3)

        by_early(drain)
        sent(whole_out, 4)

    @pl.when(me == 2)
    def _():
        def start(h):
            move(
                q_ref.at[:, cols(h)], qq.at[0, :, cols(h)], sem_s.at[0], sem_b.at[h], 1
            ).start()

        def relay(h):
            start(h)
            q3 = qq.at[1, :, cols(h)]
            arrived(q3, sem_b.at[h])
            move(q3, q3, sem_s.at[5], sem_b.at[h], 1).start()

        each(early, early + DIRECT, start)
        each(early + DIRECT, whole, relay)
        for c in range(count):
            for i, src, sem in ((0, k_ref, c), (1, v_ref, c), (5, q_ref, count + c)):
                to_whole(c, i, src, sem)

        wait_loads()

        def pass_on(h, level, out):
            pack_s[h, :HEAD] = out.astype(jnp.bfloat16)
            st_s[h, 0:1] = level
            st_s[h, 1:2] = level
            pack_right(h, 2, 3)
            st_right(h, 3, 3)

        def early_head(h):
            q, k, v = own_qkv(h)
            arrived(early_kv.at[:, h], sem_a.at[h])
            arrived(qq.at[1, :, cols(h)], sem_b.at[h])
            k0, v0, k1, v1 = [early_kv[i, h] for i in range(4)]
            phi_k = feature_map(k)
            before = tn(feature_map(k0), v0) + tn(feature_map(k1), v1)
            put_state(h, before + tn(phi_k, v))
            q3 = qq[1, :, cols(h)]
            other = soft([nt(k0, q3), nt(k1, q3), nt(k, q3)], [v0, v1, v])
            pass_on(h, *normalised(other))
            phi_q, linear = local_linear(q, phi_k, v)
            linear = linear + tt(before.astype(jnp.bfloat16), phi_q)
            scores = [nt(k0, q), nt(k1, q), diagonal(q, k)]
            finish(h, soft(scores, [v0, v1, v]), linear)

        each(0, early, early_head)

        def for_last(h):
            k, v = own[1, :, cols(h)], own[2, :, cols(h)]
            state = tn(feature_map(k), v)

            @pl.when(h < early + DIRECT)
            def _():
                arrived(qq.at[1, :, cols(h)], sem_w.at[spare + h - early])

            other = soft([nt(k, qq[1, :, cols(h)])], [v])
            pack_arrived(h)
            put_state(h, get_state(h).astype(jnp.float32) + state)
            pass_on(h, *normalised(merge(other, st_r[h, 1:2], pack_r[h, :HEAD])))

        def for_own(h):
            q, k, v = own_qkv(h)
            phi_q, linear = local_linear(q, feature_map(k), v)
            linear = linear + tt(get_state(h), phi_q)
            own_sum = soft([diagonal(q, k)], [v])
            arrived(oa_r.at[h], sem_b.at[h])
            finish(h, merge(own_sum, st_r[h, 0:1], oa_r[h]), linear)

        def head(h):
            for_last(h)
            in_turn(h, for_own)

        each(early, whole, head)
        each(whole - lag, whole, for_own)


        def drain(count):
            sent(qq.at[0, :, count * HEAD : whole * HEAD], 0)
            sent(qq.at[1, :, (count + DIRECT) * HEAD : whole * HEAD], 5)

        by_early(drain)
        sent(whole_in.at[:, 0:3], 1)
        sent(pack_s.at[0:whole], 2)
        sent(st_s.at[0:whole], 3)
        arrived(out_ref.at[:, whole * HEAD :], sem_w.at[2 * count])

    @pl.when(me == 3)
    def _():
        def to_hub(h):
            move(
                q_ref.at[:, cols(h)], qq.at[1, :, cols(h)], sem_s.at[2], sem_b.at[h], 1
            ).start()

        def to_left(h, sem):
            move(q_ref.at[:, cols(h)], qq.at[1, :, cols(h)], sem_s.at[0], sem, 2).start()

        each(early, early + DIRECT, to_hub)
        each(early + DIRECT, whole, lambda h: to_left(h, sem_b.at[h]))
        each(0, early, lambda h: to_left(h, sem_b.at[h]))
        each(0, DIRECT, lambda i: to_left(early + i, sem_w.at[spare + i]))

        wait_loads()

        def compute(h):
            q, k, v = own_qkv(h)
            phi_q, linear = local_linear(q, feature_map(k), v)
            own_sum = soft([diagonal(q, k)], [v])
            pack_arrived(h)
            linear = linear + tt(get_state(h), phi_q)
            finish(h, merge(own_sum, st_r[h, 0:1], pack_r[h, :HEAD]), linear)

        each(0, turn, compute)
        for c in range(count):
            for i, src in enumerate((q_ref, k_ref, v_ref)):
                to_whole(c, 2 + i, src, c)
        each(turn, whole, compute)

        sent(qq.at[1, :, : whole * HEAD], 0)
        sent(whole_in.at[:, 0:3], 1)
        by_early(lambda count: sent(qq.at[1, :, count * HEAD : (count + DIRECT) * HEAD], 2))
        arrived(out_ref.at[:, whole * HEAD :], sem_w.at[2 * count])


def hub_shards(queries, key_vectors, value_vectors, norm_gain, window_gain):
    tok, width = queries.shape
    heads = width // HEAD
    most, _, _, whole = classes(heads)
    count = heads - whole
    hbm = pl.BlockSpec(memory_space=pl.ANY)
    pack = pltpu.VMEM((heads, HEAD + HEAD * HEAD // tok, tok), jnp.bfloat16)
    partial = pltpu.VMEM((heads, HEAD, tok), jnp.bfloat16)
    stats = pltpu.VMEM((heads, 2, tok), jnp.float32)
    dma = pltpu.SemaphoreType.DMA
    return pl.pallas_call(
        hub_kernel,
        out_shape=pltpu.VMEM((tok, width), jnp.bfloat16),
        in_specs=[hbm] * 5,
        out_specs=pl.BlockSpec(memory_space=pltpu.VMEM),
        scratch_shapes=[
            pltpu.VMEM((2, tok, width), jnp.bfloat16),
            pltpu.VMEM((2, tok, width), jnp.bfloat16),
            pltpu.VMEM((3, tok, width), jnp.bfloat16),
            pltpu.VMEM((2, heads, HEAD), jnp.float32),
            pltpu.VMEM((4, most, tok, HEAD), jnp.bfloat16),
            pltpu.VMEM((count, 6, tok, HEAD), jnp.bfloat16),
            pltpu.VMEM((count, 2, tok, HEAD), jnp.bfloat16),
        ]
        + [pack] * 2
        + [partial] * 2
        + [stats] * 2
        + [pltpu.VMEM(((HEAD + HEAD * HEAD // tok) // 4 + 1, 2, tok), jnp.float32)]
        + [dma((heads,))] * 2
        + [dma((2 * count + 1 + DIRECT,)), dma((6,)), dma((2,))],
        compiler_params=pltpu.CompilerParams(
            collective_id=0, has_side_effects=True, vmem_limit_bytes=56 * 2**20
        ),
        name="hub_attention",
    )(
        queries,
        key_vectors,
        value_vectors,
        norm_gain.reshape(heads, HEAD),
        window_gain.reshape(heads, HEAD),
    )


def solution(mesh):
    count = mesh.shape["ctx"]

    def run(queries, key_vectors, value_vectors, norm_gain, window_gain):
        args = (queries, key_vectors, value_vectors, norm_gain, window_gain)
        fits = count * queries.shape[0] <= WINDOW
        tok, width = queries.shape
        even = tok % HEAD == 0 and HEAD * HEAD % (16 * tok) == 0
        if fits and even and count == 4 and width >= 16 * HEAD:
            return hub_shards(*args)
        return shards(*args)

    return jax.shard_map(
        run,
        mesh=mesh,
        in_specs=(P(("dp", "ctx"), None), P(("dp", "ctx"), None), P(("dp", "ctx"), None), P(), P()),
        out_specs=P(("dp", "ctx"), None),
        check_vma=False,
    )
```

```python
import functools
import math

import jax
import jax.numpy as jnp
from jax import lax
from jax.experimental import pallas as pl
from jax.experimental.pallas import tpu as pltpu
from jax.sharding import PartitionSpec as P

HEAD = 128
WINDOW = 1024
EPS = 1e-05


def passed_along(value, axis, steps):
    count = lax.axis_size(axis)
    leading, last = (max(0, -steps), min(count, count - steps))
    return lax.ppermute(value, axis, [(source, source + steps) for source in range(leading, last)])


def entering(array, axis, combine, identity):
    peers, position = (lax.axis_size(axis), lax.axis_index(axis))
    everything = lax.all_gather(array.astype(jnp.bfloat16), axis)
    start = jnp.broadcast_to(jnp.asarray(identity, array.dtype), array.shape)

    def lap(k, before):
        reached = k < position
        new = combine(before, everything[k].astype(array.dtype))
        return jnp.where(reached, new, before)

    return lax.fori_loop(0, peers, lap, start)


def feature_map(values):
    upcast = values.astype(jnp.float32)
    return jnp.where(upcast > 0, upcast + 1.0, jnp.exp(jnp.minimum(upcast, 0.0))).astype(
        jnp.bfloat16
    )


def add_states(earlier, later):
    return earlier + later


def shards(queries, key_vectors, value_vectors, norm_gain, window_gain):
    tok_rows, model_width = queries.shape
    head_count = model_width // HEAD
    ctx_index = lax.axis_index("ctx")
    reach_blocks = WINDOW // tok_rows
    own_pair = (key_vectors, value_vectors)
    received = []
    travelling = own_pair
    for distance in range(reach_blocks):
        travelling = passed_along((travelling[0], travelling[1]), "ctx", 1)
        received.append(travelling)
    ordered = received[::-1] + [own_pair]
    window_keys = jnp.concatenate([member[0] for member in ordered], axis=0)
    window_values = jnp.concatenate([member[1] for member in ordered], axis=0)
    span_rows = window_keys.shape[0]
    query_place = ctx_index * tok_rows + jnp.arange(tok_rows, dtype=jnp.int32)
    key_place = (ctx_index - reach_blocks) * tok_rows + jnp.arange(span_rows, dtype=jnp.int32)
    inside = (
        (key_place[None, :] <= query_place[:, None])
        & (query_place[:, None] - key_place[None, :] < WINDOW)
        & (key_place[None, :] >= 0)
    )
    group_size = 4
    groups = head_count // group_size
    scale = 1.0 / math.sqrt(HEAD)

    def split_groups(matrix):
        return jnp.moveaxis(matrix.reshape(matrix.shape[0], groups, group_size, HEAD), 1, 0)

    def attend(operands):
        query_group, key_group, value_group = operands
        scores = (
            jnp.einsum("tge,sge->gts", query_group, key_group, preferred_element_type=jnp.float32)
            * scale
        )
        scores = jnp.where(inside[None], scores, -jnp.inf)
        peak = jnp.max(scores, axis=-1, keepdims=True)
        expos = jnp.exp(scores - peak)
        weights = (expos / jnp.sum(expos, axis=-1, keepdims=True)).astype(jnp.bfloat16)
        return jnp.einsum("gts,sge->tge", weights, value_group, preferred_element_type=jnp.float32)

    attended = lax.map(
        attend, (split_groups(queries), split_groups(window_keys), split_groups(window_values))
    )
    attended = jnp.moveaxis(attended, 0, 1).reshape(tok_rows, head_count, HEAD)
    windowed = attended * lax.rsqrt(jnp.mean(attended * attended, axis=-1, keepdims=True) + EPS)
    windowed = windowed * window_gain.reshape(head_count, HEAD)
    phi_query = feature_map(queries).reshape(tok_rows, head_count, HEAD)
    phi_key = feature_map(key_vectors).reshape(tok_rows, head_count, HEAD)
    value_heads = value_vectors.reshape(tok_rows, head_count, HEAD)
    local_state = jnp.einsum(
        "the,thf->hef", phi_key, value_heads, preferred_element_type=jnp.float32
    )
    carried = entering(local_state, "ctx", add_states, jnp.zeros_like(local_state))
    from_state = jnp.einsum(
        "the,hef->thf", phi_query, carried.astype(jnp.bfloat16), preferred_element_type=jnp.float32
    )
    affinity = jnp.einsum("the,she->hts", phi_query, phi_key, preferred_element_type=jnp.float32)
    inner = jnp.arange(tok_rows, dtype=jnp.int32)
    causal = inner[:, None] >= inner[None, :]
    affinity = jnp.where(causal[None], affinity, 0.0).astype(jnp.bfloat16)
    local_part = jnp.einsum(
        "hts,shf->thf", affinity, value_heads, preferred_element_type=jnp.float32
    )
    linear = from_state + local_part
    normed = linear * lax.rsqrt(jnp.mean(linear * linear, axis=-1, keepdims=True) + EPS)
    normed = normed * norm_gain.reshape(head_count, HEAD)
    return (windowed + normed).reshape(tok_rows, model_width).astype(jnp.bfloat16)


EXP_SCALE = math.log2(math.e) / math.sqrt(HEAD)
LOW = -1e30


def nt(a, b):
    return lax.dot_general(a, b, (((1,), (1,)), ((), ())), preferred_element_type=jnp.float32)


def tn(a, b):
    return lax.dot_general(a, b, (((0,), (0,)), ((), ())), preferred_element_type=jnp.float32)


def tt(a, b):
    return lax.dot_general(a, b, (((0,), (1,)), ((), ())), preferred_element_type=jnp.float32)


DIRECT = 2


def classes(heads):
    return heads // 8, heads // 16, heads // 2, heads - heads // 8


def hub_kernel(
    q_ref, k_ref, v_ref, gn_ref, gw_ref, out_ref,
    kv0, qq, own, gains, early_kv, whole_in, whole_out, pack_s, pack_r, oa_s, oa_r, st_s, st_r,
    tally, sem_a, sem_b, sem_w, sem_s, loaded,
):
    tok, width = q_ref.shape
    heads = width // HEAD
    most, least, cut, whole = classes(heads)
    count = heads - whole
    half = tok - tok // 4
    depth = HEAD * HEAD // tok
    me = lax.axis_index("ctx")
    fewer = lax.rem(lax.axis_index("dp"), 2)
    early = most + fewer * (least - most)
    spare = 2 * count + 1
    turn = 7
    lag = 2
    MESH = pl.DeviceIdType.MESH

    def cols(h):
        if isinstance(h, int):
            return pl.ds(h * HEAD, HEAD)
        return pl.ds(pl.multiple_of(h * HEAD, HEAD), HEAD)

    def move(src, dst, sent, arrived, target):
        return pltpu.make_async_remote_copy(
            src_ref=src,
            dst_ref=dst,
            send_sem=sent,
            recv_sem=arrived,
            device_id={"ctx": target},
            device_id_type=MESH,
        )

    def arrived(ref, sem):
        move(ref, ref, sem_s.at[0], sem, 0).wait_recv()

    def sent(ref, i):
        move(ref, ref, sem_s.at[i], sem_w.at[0], 0).wait_send()

    def to_whole(c, i, src, sem):
        move(
            src.at[:, cols(whole + c)], whole_in.at[c, i], sem_s.at[1], sem_w.at[sem], 1
        ).start()

    def each(start, stop, body):
        def step(h, carry):
            body(h)
            return carry

        lax.fori_loop(start, stop, step, 0)

    def by_early(body):
        for which, count in enumerate((most, least)):

            @pl.when(fewer == which)
            def _():
                body(count)

    skips = [cut + 2 * i for i in range(lag)]

    def in_turn(h, body):
        late = sum((h >= at).astype(jnp.int32) for at in skips)

        @pl.when(functools.reduce(jnp.logical_and, [h != at for at in skips]))
        def _():
            body(h - late)

    loads = [
        pltpu.make_async_copy(src, own.at[i], loaded.at[0])
        for i, src in enumerate([q_ref, k_ref, v_ref])
    ] + [
        pltpu.make_async_copy(src, gains.at[i], loaded.at[1])
        for i, src in enumerate([gn_ref, gw_ref])
    ]
    for load in loads:
        load.start()

    def wait_loads():
        pltpu.make_async_copy(own, own, loaded.at[0]).wait()
        pltpu.make_async_copy(gains, gains, loaded.at[1]).wait()

    barrier = pltpu.get_barrier_semaphore()
    senders = {1: (0, 2, 3), 2: (1, 3)}
    for device, others in senders.items():

        @pl.when(me == device)
        def _():
            for other in others:
                pl.semaphore_signal(
                    barrier, inc=1, device_id={"ctx": other}, device_id_type=MESH
                )

    pl.semaphore_wait(barrier, 1 + (me == 3).astype(jnp.int32))

    key_at = lax.broadcasted_iota(jnp.int32, (tok, tok), 0)
    query_at = lax.broadcasted_iota(jnp.int32, (tok, tok), 1)
    causal = key_at <= query_at

    def own_qkv(h):
        return own[0, :, cols(h)], own[1, :, cols(h)], own[2, :, cols(h)]

    def soft(scores, values):
        peak = functools.reduce(
            jnp.maximum, [jnp.max(s, axis=0, keepdims=True) for s in scores]
        )
        total, out = 0.0, 0.0
        for s, v in zip(scores, values):
            e = jnp.exp2((s - peak) * EXP_SCALE)
            total = total + jnp.sum(e, axis=0, keepdims=True)
            out = out + tn(v, e.astype(jnp.bfloat16))
        return peak, total, out

    def normalised(soft_sum):
        peak, total, out = soft_sum
        return peak + jnp.log2(total) * (1.0 / EXP_SCALE), out * (1.0 / total)

    def merge(one, level, out):
        top = jnp.maximum(one[0], level)
        f1 = jnp.exp2((one[0] - top) * EXP_SCALE)
        f2 = jnp.exp2((level - top) * EXP_SCALE)
        return top, one[1] * f1 + f2, one[2] * f1 + out.astype(jnp.float32) * f2

    def local_linear(q, phi_k, v):
        phi_q = feature_map(q)
        affinity = jnp.where(causal, nt(phi_k, phi_q), 0.0).astype(jnp.bfloat16)
        return phi_q, tn(v, affinity)

    def rows_of(h, soft_sum, linear):
        _, total, out = soft_sum
        att = out * (1.0 / total)
        att = att * lax.rsqrt(jnp.mean(att * att, axis=0, keepdims=True) + EPS)
        lin = linear * lax.rsqrt(jnp.mean(linear * linear, axis=0, keepdims=True) + EPS)
        row = att.T * gains[1, pl.ds(h, 1), :] + lin.T * gains[0, pl.ds(h, 1), :]
        return row.astype(jnp.bfloat16)

    def finish(h, soft_sum, linear):
        out_ref[:, cols(h)] = rows_of(h, soft_sum, linear)

    def diagonal(q, k):
        return jnp.where(causal, nt(k, q), LOW)

    def put_state(h, state):
        for i in range(tok // HEAD):
            pack_s[h, HEAD : HEAD + depth, i * HEAD : (i + 1) * HEAD] = state[
                i * depth : (i + 1) * depth
            ].astype(jnp.bfloat16)

    def get_state(h):
        pieces = [
            pack_r[h, HEAD : HEAD + depth, i * HEAD : (i + 1) * HEAD] for i in range(tok // HEAD)
        ]
        return jnp.concatenate(pieces, axis=0)

    def pack_right(h, i, target):
        move(pack_s.at[h], pack_r.at[h], sem_s.at[i], sem_a.at[h], target).start()

    def st_right(h, i, target):
        move(st_s.at[h], st_r.at[h], sem_s.at[i], sem_a.at[h], target).start()

    def pack_arrived(h):
        arrived(tally, sem_a.at[h])

    @pl.when(me == 0)
    def _():
        def start(h):
            for i, src in enumerate((k_ref, v_ref)):
                move(
                    src.at[:, cols(h)], kv0.at[i, :, cols(h)], sem_s.at[0], sem_a.at[h], 1
                ).start()

        each(0, heads, start)

        wait_loads()

        def compute(h):
            q, k, v = own_qkv(h)
            _, linear = local_linear(q, feature_map(k), v)
            finish(h, soft([diagonal(q, k)], [v]), linear)

        each(0, heads, compute)
        sent(kv0, 0)

    @pl.when(me == 1)
    def _():
        def to_early(i, src, h):
            move(src, early_kv.at[i, h], sem_s.at[0], sem_a.at[h], 2).start()

        def start(h):
            to_early(2, k_ref.at[:, cols(h)], h)
            to_early(3, v_ref.at[:, cols(h)], h)

        each(0, early, start)

        wait_loads()

        def own_rows(h, q, k, v, k0, v0, phi_k, before):
            phi_q, linear = local_linear(q, phi_k, v)
            linear = linear + tt(before.astype(jnp.bfloat16), phi_q)
            finish(h, soft([nt(k0, q), diagonal(q, k)], [v0, v]), linear)

        def early_head(h):
            q, k, v = own_qkv(h)
            arrived(kv0.at[:, :, cols(h)], sem_a.at[h])
            to_early(0, kv0.at[0, :, cols(h)], h)
            to_early(1, kv0.at[1, :, cols(h)], h)
            k0, v0 = kv0[0, :, cols(h)], kv0[1, :, cols(h)]
            before = tn(feature_map(k0), v0)
            own_rows(h, q, k, v, k0, v0, feature_map(k), before)

        each(0, early, early_head)

        def oa_right(h):
            move(oa_s.at[h], oa_r.at[h], sem_s.at[3], sem_b.at[h], 2).start()

        def shared_head(h):
            q, k, v = own_qkv(h)
            phi_k = feature_map(k)
            state = tn(phi_k, v)
            arrived(kv0.at[:, :, cols(h)], sem_a.at[h])
            k0, v0 = kv0[0, :, cols(h)], kv0[1, :, cols(h)]
            before = tn(feature_map(k0), v0)
            put_state(h, before + state)
            arrived(qq.at[:, :, cols(h)], sem_b.at[h])

            def part(i):
                other = qq[i, :, cols(h)]
                level, out = normalised(soft([nt(k0, other), nt(k, other)], [v0, v]))
                st_s[h, i : i + 1] = level
                return out.astype(jnp.bfloat16)

            pack_s[h, :HEAD] = part(1)
            pack_right(h, 1, 2)
            oa_s[h] = part(0)
            st_right(h, 2, 2)

            in_turn(h, oa_right)
            own_rows(h, q, k, v, k0, v0, phi_k, before)

        def out_right(c, i, target, first, rows):
            move(
                whole_out.at[c, i, first : first + rows],
                out_ref.at[first : first + rows, cols(whole + c)],
                sem_s.at[4],
                sem_w.at[2 * count],
                target,
            ).start()

        def whole_head(c):
            h = whole + c
            q, k, v = own_qkv(h)
            phi_k = feature_map(k)
            arrived(kv0.at[:, :, cols(h)], sem_a.at[h])
            k0, v0 = kv0[0, :, cols(h)], kv0[1, :, cols(h)]
            before = tn(feature_map(k0), v0)
            own_rows(h, q, k, v, k0, v0, phi_k, before)
            before = before + tn(phi_k, v)
            arrived(whole_in.at[c, 0:5], sem_w.at[c])
            k2, v2, q3, k3, v3 = [whole_in[c, i] for i in range(5)]
            phi_k2 = feature_map(k2)
            after = before + tn(phi_k2, v2)
            phi_q, linear = local_linear(q3, feature_map(k3), v3)
            linear = linear + tt(after.astype(jnp.bfloat16), phi_q)
            scores = [nt(k0, q3), nt(k, q3), nt(k2, q3), diagonal(q3, k3)]
            whole_out[c, 1] = rows_of(h, soft(scores, [v0, v, v2, v3]), linear)
            out_right(c, 1, 3, 0, half)
            arrived(whole_in.at[c, 5], sem_w.at[count + c])
            q2 = whole_in[c, 5]
            phi_q, linear = local_linear(q2, phi_k2, v2)
            linear = linear + tt(before.astype(jnp.bfloat16), phi_q)
            scores = [nt(k0, q2), nt(k, q2), diagonal(q2, k2)]
            whole_out[c, 0] = rows_of(h, soft(scores, [v0, v, v2]), linear)
            out_right(c, 0, 2, 0, tok)
            out_right(c, 1, 3, half, tok - half)

        each(early, whole, shared_head)
        each(whole - lag, whole, oa_right)
        each(0, count, whole_head)

        def drain(count):
            sent(early_kv.at[:, 0:count], 0)
            sent(pack_s.at[count:whole], 1)
            sent(st_s.at[count:whole], 2)
            sent(oa_s.at[count:whole], 3)

        by_early(drain)
        sent(whole_out, 4)

    @pl.when(me == 2)
    def _():
        def start(h):
            move(
                q_ref.at[:, cols(h)], qq.at[0, :, cols(h)], sem_s.at[0], sem_b.at[h], 1
            ).start()

        def relay(h):
            start(h)
            q3 = qq.at[1, :, cols(h)]
            arrived(q3, sem_b.at[h])
            move(q3, q3, sem_s.at[5], sem_b.at[h], 1).start()

        each(early, early + DIRECT, start)
        each(early + DIRECT, whole, relay)
        for c in range(count):
            for i, src, sem in ((0, k_ref, c), (1, v_ref, c), (5, q_ref, count + c)):
                to_whole(c, i, src, sem)

        wait_loads()

        def pass_on(h, level, out):
            pack_s[h, :HEAD] = out.astype(jnp.bfloat16)
            st_s[h, 0:1] = level
            st_s[h, 1:2] = level
            pack_right(h, 2, 3)
            st_right(h, 3, 3)

        def early_head(h):
            q, k, v = own_qkv(h)
            arrived(early_kv.at[:, h], sem_a.at[h])
            arrived(qq.at[1, :, cols(h)], sem_b.at[h])
            k0, v0, k1, v1 = [early_kv[i, h] for i in range(4)]
            phi_k = feature_map(k)
            before = tn(feature_map(k0), v0) + tn(feature_map(k1), v1)
            put_state(h, before + tn(phi_k, v))
            q3 = qq[1, :, cols(h)]
            other = soft([nt(k0, q3), nt(k1, q3), nt(k, q3)], [v0, v1, v])
            pass_on(h, *normalised(other))
            phi_q, linear = local_linear(q, phi_k, v)
            linear = linear + tt(before.astype(jnp.bfloat16), phi_q)
            scores = [nt(k0, q), nt(k1, q), diagonal(q, k)]
            finish(h, soft(scores, [v0, v1, v]), linear)

        each(0, early, early_head)

        def for_last(h):
            k, v = own[1, :, cols(h)], own[2, :, cols(h)]
            state = tn(feature_map(k), v)

            @pl.when(h < early + DIRECT)
            def _():
                arrived(qq.at[1, :, cols(h)], sem_w.at[spare + h - early])

            other = soft([nt(k, qq[1, :, cols(h)])], [v])
            pack_arrived(h)
            put_state(h, get_state(h).astype(jnp.float32) + state)
            pass_on(h, *normalised(merge(other, st_r[h, 1:2], pack_r[h, :HEAD])))

        def for_own(h):
            q, k, v = own_qkv(h)
            phi_q, linear = local_linear(q, feature_map(k), v)
            linear = linear + tt(get_state(h), phi_q)
            own_sum = soft([diagonal(q, k)], [v])
            arrived(oa_r.at[h], sem_b.at[h])
            finish(h, merge(own_sum, st_r[h, 0:1], oa_r[h]), linear)

        def head(h):
            for_last(h)
            in_turn(h, for_own)

        each(early, whole, head)
        each(whole - lag, whole, for_own)
        arrived(out_ref.at[:, whole * HEAD :], sem_w.at[2 * count])


        def drain(count):
            sent(qq.at[0, :, count * HEAD : whole * HEAD], 0)
            sent(qq.at[1, :, (count + DIRECT) * HEAD : whole * HEAD], 5)

        by_early(drain)
        sent(whole_in.at[:, 0:3], 1)
        sent(pack_s.at[0:whole], 2)
        sent(st_s.at[0:whole], 3)

    @pl.when(me == 3)
    def _():
        def to_hub(h):
            move(
                q_ref.at[:, cols(h)], qq.at[1, :, cols(h)], sem_s.at[2], sem_b.at[h], 1
            ).start()

        def to_left(h, sem):
            move(q_ref.at[:, cols(h)], qq.at[1, :, cols(h)], sem_s.at[0], sem, 2).start()

        each(early, early + DIRECT, to_hub)
        each(early + DIRECT, whole, lambda h: to_left(h, sem_b.at[h]))
        each(0, early, lambda h: to_left(h, sem_b.at[h]))
        each(0, DIRECT, lambda i: to_left(early + i, sem_w.at[spare + i]))

        wait_loads()

        def compute(h):
            q, k, v = own_qkv(h)
            phi_q, linear = local_linear(q, feature_map(k), v)
            own_sum = soft([diagonal(q, k)], [v])
            pack_arrived(h)
            linear = linear + tt(get_state(h), phi_q)
            finish(h, merge(own_sum, st_r[h, 0:1], pack_r[h, :HEAD]), linear)

        each(0, turn, compute)
        for c in range(count):
            for i, src in enumerate((q_ref, k_ref, v_ref)):
                to_whole(c, 2 + i, src, c)
        each(turn, whole, compute)
        arrived(out_ref.at[:, whole * HEAD :], sem_w.at[2 * count])

        sent(qq.at[1, :, : whole * HEAD], 0)
        sent(whole_in.at[:, 0:3], 1)
        by_early(lambda count: sent(qq.at[1, :, count * HEAD : (count + DIRECT) * HEAD], 2))


def hub_shards(queries, key_vectors, value_vectors, norm_gain, window_gain):
    tok, width = queries.shape
    heads = width // HEAD
    most, _, _, whole = classes(heads)
    count = heads - whole
    hbm = pl.BlockSpec(memory_space=pl.ANY)
    pack = pltpu.VMEM((heads, HEAD + HEAD * HEAD // tok, tok), jnp.bfloat16)
    partial = pltpu.VMEM((heads, HEAD, tok), jnp.bfloat16)
    stats = pltpu.VMEM((heads, 2, tok), jnp.float32)
    dma = pltpu.SemaphoreType.DMA
    return pl.pallas_call(
        hub_kernel,
        out_shape=pltpu.VMEM((tok, width), jnp.bfloat16),
        in_specs=[hbm] * 5,
        out_specs=pl.BlockSpec(memory_space=pltpu.VMEM),
        scratch_shapes=[
            pltpu.VMEM((2, tok, width), jnp.bfloat16),
            pltpu.VMEM((2, tok, width), jnp.bfloat16),
            pltpu.VMEM((3, tok, width), jnp.bfloat16),
            pltpu.VMEM((2, heads, HEAD), jnp.float32),
            pltpu.VMEM((4, most, tok, HEAD), jnp.bfloat16),
            pltpu.VMEM((count, 6, tok, HEAD), jnp.bfloat16),
            pltpu.VMEM((count, 2, tok, HEAD), jnp.bfloat16),
        ]
        + [pack] * 2
        + [partial] * 2
        + [stats] * 2
        + [pltpu.VMEM(((HEAD + HEAD * HEAD // tok) // 4 + 1, 2, tok), jnp.float32)]
        + [dma((heads,))] * 2
        + [dma((2 * count + 1 + DIRECT,)), dma((6,)), dma((2,))],
        compiler_params=pltpu.CompilerParams(
            collective_id=0, has_side_effects=True, vmem_limit_bytes=56 * 2**20
        ),
        name="hub_attention",
    )(
        queries,
        key_vectors,
        value_vectors,
        norm_gain.reshape(heads, HEAD),
        window_gain.reshape(heads, HEAD),
    )


def solution(mesh):
    count = mesh.shape["ctx"]

    def run(queries, key_vectors, value_vectors, norm_gain, window_gain):
        args = (queries, key_vectors, value_vectors, norm_gain, window_gain)
        fits = count * queries.shape[0] <= WINDOW
        tok, width = queries.shape
        even = tok % HEAD == 0 and HEAD * HEAD % (16 * tok) == 0
        if fits and even and count == 4 and width >= 16 * HEAD:
            return hub_shards(*args)
        return shards(*args)

    return jax.shard_map(
        run,
        mesh=mesh,
        in_specs=(P(("dp", "ctx"), None), P(("dp", "ctx"), None), P(("dp", "ctx"), None), P(), P()),
        out_specs=P(("dp", "ctx"), None),
        check_vma=False,
    )
```

```python
import functools
import math

import jax
import jax.numpy as jnp
from jax import lax
from jax.experimental import pallas as pl
from jax.experimental.pallas import tpu as pltpu
from jax.sharding import PartitionSpec as P

HEAD = 128
WINDOW = 1024
EPS = 1e-05


def passed_along(value, axis, steps):
    count = lax.axis_size(axis)
    leading, last = (max(0, -steps), min(count, count - steps))
    return lax.ppermute(value, axis, [(source, source + steps) for source in range(leading, last)])


def entering(array, axis, combine, identity):
    peers, position = (lax.axis_size(axis), lax.axis_index(axis))
    everything = lax.all_gather(array.astype(jnp.bfloat16), axis)
    start = jnp.broadcast_to(jnp.asarray(identity, array.dtype), array.shape)

    def lap(k, before):
        reached = k < position
        new = combine(before, everything[k].astype(array.dtype))
        return jnp.where(reached, new, before)

    return lax.fori_loop(0, peers, lap, start)


def feature_map(values):
    upcast = values.astype(jnp.float32)
    return jnp.where(upcast > 0, upcast + 1.0, jnp.exp(jnp.minimum(upcast, 0.0))).astype(
        jnp.bfloat16
    )


def add_states(earlier, later):
    return earlier + later


def shards(queries, key_vectors, value_vectors, norm_gain, window_gain):
    tok_rows, model_width = queries.shape
    head_count = model_width // HEAD
    ctx_index = lax.axis_index("ctx")
    reach_blocks = WINDOW // tok_rows
    own_pair = (key_vectors, value_vectors)
    received = []
    travelling = own_pair
    for distance in range(reach_blocks):
        travelling = passed_along((travelling[0], travelling[1]), "ctx", 1)
        received.append(travelling)
    ordered = received[::-1] + [own_pair]
    window_keys = jnp.concatenate([member[0] for member in ordered], axis=0)
    window_values = jnp.concatenate([member[1] for member in ordered], axis=0)
    span_rows = window_keys.shape[0]
    query_place = ctx_index * tok_rows + jnp.arange(tok_rows, dtype=jnp.int32)
    key_place = (ctx_index - reach_blocks) * tok_rows + jnp.arange(span_rows, dtype=jnp.int32)
    inside = (
        (key_place[None, :] <= query_place[:, None])
        & (query_place[:, None] - key_place[None, :] < WINDOW)
        & (key_place[None, :] >= 0)
    )
    group_size = 4
    groups = head_count // group_size
    scale = 1.0 / math.sqrt(HEAD)

    def split_groups(matrix):
        return jnp.moveaxis(matrix.reshape(matrix.shape[0], groups, group_size, HEAD), 1, 0)

    def attend(operands):
        query_group, key_group, value_group = operands
        scores = (
            jnp.einsum("tge,sge->gts", query_group, key_group, preferred_element_type=jnp.float32)
            * scale
        )
        scores = jnp.where(inside[None], scores, -jnp.inf)
        peak = jnp.max(scores, axis=-1, keepdims=True)
        expos = jnp.exp(scores - peak)
        weights = (expos / jnp.sum(expos, axis=-1, keepdims=True)).astype(jnp.bfloat16)
        return jnp.einsum("gts,sge->tge", weights, value_group, preferred_element_type=jnp.float32)

    attended = lax.map(
        attend, (split_groups(queries), split_groups(window_keys), split_groups(window_values))
    )
    attended = jnp.moveaxis(attended, 0, 1).reshape(tok_rows, head_count, HEAD)
    windowed = attended * lax.rsqrt(jnp.mean(attended * attended, axis=-1, keepdims=True) + EPS)
    windowed = windowed * window_gain.reshape(head_count, HEAD)
    phi_query = feature_map(queries).reshape(tok_rows, head_count, HEAD)
    phi_key = feature_map(key_vectors).reshape(tok_rows, head_count, HEAD)
    value_heads = value_vectors.reshape(tok_rows, head_count, HEAD)
    local_state = jnp.einsum(
        "the,thf->hef", phi_key, value_heads, preferred_element_type=jnp.float32
    )
    carried = entering(local_state, "ctx", add_states, jnp.zeros_like(local_state))
    from_state = jnp.einsum(
        "the,hef->thf", phi_query, carried.astype(jnp.bfloat16), preferred_element_type=jnp.float32
    )
    affinity = jnp.einsum("the,she->hts", phi_query, phi_key, preferred_element_type=jnp.float32)
    inner = jnp.arange(tok_rows, dtype=jnp.int32)
    causal = inner[:, None] >= inner[None, :]
    affinity = jnp.where(causal[None], affinity, 0.0).astype(jnp.bfloat16)
    local_part = jnp.einsum(
        "hts,shf->thf", affinity, value_heads, preferred_element_type=jnp.float32
    )
    linear = from_state + local_part
    normed = linear * lax.rsqrt(jnp.mean(linear * linear, axis=-1, keepdims=True) + EPS)
    normed = normed * norm_gain.reshape(head_count, HEAD)
    return (windowed + normed).reshape(tok_rows, model_width).astype(jnp.bfloat16)


EXP_SCALE = math.log2(math.e) / math.sqrt(HEAD)
LOW = -1e30


def nt(a, b):
    return lax.dot_general(a, b, (((1,), (1,)), ((), ())), preferred_element_type=jnp.float32)


def tn(a, b):
    return lax.dot_general(a, b, (((0,), (0,)), ((), ())), preferred_element_type=jnp.float32)


def tt(a, b):
    return lax.dot_general(a, b, (((0,), (1,)), ((), ())), preferred_element_type=jnp.float32)


DIRECT = 2


def classes(heads):
    return heads // 8, heads // 16, heads // 2, heads - heads // 8


def hub_kernel(
    q_ref, k_ref, v_ref, gn_ref, gw_ref, out_ref,
    kv0, qq, own, gains, early_kv, whole_in, whole_out, pack_s, pack_r, oa_s, oa_r, st_s, st_r,
    tally, sem_a, sem_b, sem_w, sem_s, loaded,
):
    tok, width = q_ref.shape
    heads = width // HEAD
    most, least, cut, whole = classes(heads)
    count = heads - whole
    half = tok - tok // 4
    depth = HEAD * HEAD // tok
    me = lax.axis_index("ctx")
    fewer = lax.rem(lax.axis_index("dp"), 2)
    early = most + fewer * (least - most)
    spare = 2 * count + 1
    turn = 7
    lag = 2
    MESH = pl.DeviceIdType.MESH

    def cols(h):
        if isinstance(h, int):
            return pl.ds(h * HEAD, HEAD)
        return pl.ds(pl.multiple_of(h * HEAD, HEAD), HEAD)

    def move(src, dst, sent, arrived, target):
        return pltpu.make_async_remote_copy(
            src_ref=src,
            dst_ref=dst,
            send_sem=sent,
            recv_sem=arrived,
            device_id={"ctx": target},
            device_id_type=MESH,
        )

    def arrived(ref, sem):
        move(ref, ref, sem_s.at[0], sem, 0).wait_recv()

    def sent(ref, i):
        move(ref, ref, sem_s.at[i], sem_w.at[0], 0).wait_send()

    def to_whole(c, i, src, sem):
        move(
            src.at[:, cols(whole + c)], whole_in.at[c, i], sem_s.at[1], sem_w.at[sem], 1
        ).start()

    def each(start, stop, body):
        def step(h, carry):
            body(h)
            return carry

        lax.fori_loop(start, stop, step, 0)

    def by_early(body):
        for which, count in enumerate((most, least)):

            @pl.when(fewer == which)
            def _():
                body(count)

    skips = [cut + 2 * i for i in range(lag)]

    def in_turn(h, body):
        late = sum((h >= at).astype(jnp.int32) for at in skips)

        @pl.when(functools.reduce(jnp.logical_and, [h != at for at in skips]))
        def _():
            body(h - late)

    loads = [
        pltpu.make_async_copy(src, own.at[i], loaded.at[0])
        for i, src in enumerate([q_ref, k_ref, v_ref])
    ] + [
        pltpu.make_async_copy(src, gains.at[i], loaded.at[1])
        for i, src in enumerate([gn_ref, gw_ref])
    ]
    for load in loads:
        load.start()

    def wait_loads():
        pltpu.make_async_copy(own, own, loaded.at[0]).wait()
        pltpu.make_async_copy(gains, gains, loaded.at[1]).wait()

    barrier = pltpu.get_barrier_semaphore()
    senders = {1: (0, 2, 3), 2: (1, 3)}
    for device, others in senders.items():

        @pl.when(me == device)
        def _():
            for other in others:
                pl.semaphore_signal(
                    barrier, inc=1, device_id={"ctx": other}, device_id_type=MESH
                )

    pl.semaphore_wait(barrier, 1 + (me == 3).astype(jnp.int32))

    key_at = lax.broadcasted_iota(jnp.int32, (tok, tok), 0)
    query_at = lax.broadcasted_iota(jnp.int32, (tok, tok), 1)
    causal = key_at <= query_at

    def own_qkv(h):
        return own[0, :, cols(h)], own[1, :, cols(h)], own[2, :, cols(h)]

    def soft(scores, values):
        peak = functools.reduce(
            jnp.maximum, [jnp.max(s, axis=0, keepdims=True) for s in scores]
        )
        total, out = 0.0, 0.0
        for s, v in zip(scores, values):
            e = jnp.exp2((s - peak) * EXP_SCALE)
            total = total + jnp.sum(e, axis=0, keepdims=True)
            out = out + tn(v, e.astype(jnp.bfloat16))
        return peak, total, out

    def normalised(soft_sum):
        peak, total, out = soft_sum
        return peak + jnp.log2(total) * (1.0 / EXP_SCALE), out * (1.0 / total)

    def merge(one, level, out):
        top = jnp.maximum(one[0], level)
        f1 = jnp.exp2((one[0] - top) * EXP_SCALE)
        f2 = jnp.exp2((level - top) * EXP_SCALE)
        return top, one[1] * f1 + f2, one[2] * f1 + out.astype(jnp.float32) * f2

    def local_linear(q, phi_k, v):
        phi_q = feature_map(q)
        affinity = jnp.where(causal, nt(phi_k, phi_q), 0.0).astype(jnp.bfloat16)
        return phi_q, tn(v, affinity)

    def rows_of(h, soft_sum, linear):
        _, total, out = soft_sum
        att = out * (1.0 / total)
        att = att * lax.rsqrt(jnp.mean(att * att, axis=0, keepdims=True) + EPS)
        lin = linear * lax.rsqrt(jnp.mean(linear * linear, axis=0, keepdims=True) + EPS)
        row = att.T * gains[1, pl.ds(h, 1), :] + lin.T * gains[0, pl.ds(h, 1), :]
        return row.astype(jnp.bfloat16)

    def finish(h, soft_sum, linear):
        out_ref[:, cols(h)] = rows_of(h, soft_sum, linear)

    def diagonal(q, k):
        return jnp.where(causal, nt(k, q), LOW)

    def put_state(h, state):
        for i in range(tok // HEAD):
            pack_s[h, HEAD : HEAD + depth, i * HEAD : (i + 1) * HEAD] = state[
                i * depth : (i + 1) * depth
            ].astype(jnp.bfloat16)

    def get_state(h):
        pieces = [
            pack_r[h, HEAD : HEAD + depth, i * HEAD : (i + 1) * HEAD] for i in range(tok // HEAD)
        ]
        return jnp.concatenate(pieces, axis=0)

    def pack_right(h, i, target):
        move(pack_s.at[h], pack_r.at[h], sem_s.at[i], sem_a.at[h], target).start()

    def st_right(h, i, target):
        move(st_s.at[h], st_r.at[h], sem_s.at[i], sem_a.at[h], target).start()

    def pack_arrived(h):
        arrived(tally, sem_a.at[h])

    @pl.when(me == 0)
    def _():
        def start(h):
            for i, src in enumerate((k_ref, v_ref)):
                move(
                    src.at[:, cols(h)], kv0.at[i, :, cols(h)], sem_s.at[0], sem_a.at[h], 1
                ).start()

        each(0, heads, start)

        wait_loads()

        def compute(h):
            q, k, v = own_qkv(h)
            _, linear = local_linear(q, feature_map(k), v)
            finish(h, soft([diagonal(q, k)], [v]), linear)

        each(0, heads, compute)
        sent(kv0, 0)

    @pl.when(me == 1)
    def _():
        def to_early(i, src, h):
            move(src, early_kv.at[i, h], sem_s.at[0], sem_a.at[h], 2).start()

        def start(h):
            to_early(2, k_ref.at[:, cols(h)], h)
            to_early(3, v_ref.at[:, cols(h)], h)

        each(0, early, start)

        wait_loads()

        def own_rows(h, q, k, v, k0, v0, phi_k, before):
            phi_q, linear = local_linear(q, phi_k, v)
            linear = linear + tt(before.astype(jnp.bfloat16), phi_q)
            finish(h, soft([nt(k0, q), diagonal(q, k)], [v0, v]), linear)

        def early_head(h):
            q, k, v = own_qkv(h)
            arrived(kv0.at[:, :, cols(h)], sem_a.at[h])
            to_early(0, kv0.at[0, :, cols(h)], h)
            to_early(1, kv0.at[1, :, cols(h)], h)
            k0, v0 = kv0[0, :, cols(h)], kv0[1, :, cols(h)]
            before = tn(feature_map(k0), v0)
            own_rows(h, q, k, v, k0, v0, feature_map(k), before)

        each(0, early, early_head)

        def oa_right(h):
            move(oa_s.at[h], oa_r.at[h], sem_s.at[3], sem_b.at[h], 2).start()

        def shared_head(h):
            q, k, v = own_qkv(h)
            phi_k = feature_map(k)
            state = tn(phi_k, v)
            arrived(kv0.at[:, :, cols(h)], sem_a.at[h])
            k0, v0 = kv0[0, :, cols(h)], kv0[1, :, cols(h)]
            before = tn(feature_map(k0), v0)
            put_state(h, before + state)
            arrived(qq.at[:, :, cols(h)], sem_b.at[h])

            def part(i):
                other = qq[i, :, cols(h)]
                level, out = normalised(soft([nt(k0, other), nt(k, other)], [v0, v]))
                st_s[h, i : i + 1] = level
                return out.astype(jnp.bfloat16)

            pack_s[h, :HEAD] = part(1)
            pack_right(h, 1, 2)
            oa_s[h] = part(0)
            st_right(h, 2, 2)

            in_turn(h, oa_right)
            own_rows(h, q, k, v, k0, v0, phi_k, before)

        def out_right(c, i, target, first, rows):
            move(
                whole_out.at[c, i, first : first + rows],
                out_ref.at[first : first + rows, cols(whole + c)],
                sem_s.at[4],
                sem_w.at[2 * count],
                target,
            ).start()

        def whole_head(c):
            h = whole + c
            q, k, v = own_qkv(h)
            phi_k = feature_map(k)
            arrived(kv0.at[:, :, cols(h)], sem_a.at[h])
            k0, v0 = kv0[0, :, cols(h)], kv0[1, :, cols(h)]
            before = tn(feature_map(k0), v0)
            own_rows(h, q, k, v, k0, v0, phi_k, before)
            before = before + tn(phi_k, v)
            arrived(whole_in.at[c, 0:5], sem_w.at[c])
            k2, v2, q3, k3, v3 = [whole_in[c, i] for i in range(5)]
            phi_k2 = feature_map(k2)
            after = before + tn(phi_k2, v2)
            phi_q, linear = local_linear(q3, feature_map(k3), v3)
            linear = linear + tt(after.astype(jnp.bfloat16), phi_q)
            scores = [nt(k0, q3), nt(k, q3), nt(k2, q3), diagonal(q3, k3)]
            whole_out[c, 1] = rows_of(h, soft(scores, [v0, v, v2, v3]), linear)
            out_right(c, 1, 3, 0, half)
            arrived(whole_in.at[c, 5], sem_w.at[count + c])
            q2 = whole_in[c, 5]
            phi_q, linear = local_linear(q2, phi_k2, v2)
            linear = linear + tt(before.astype(jnp.bfloat16), phi_q)
            scores = [nt(k0, q2), nt(k, q2), diagonal(q2, k2)]
            whole_out[c, 0] = rows_of(h, soft(scores, [v0, v, v2]), linear)
            out_right(c, 0, 2, 0, tok)
            out_right(c, 1, 3, half, tok - half)

        each(early, whole, shared_head)
        each(whole - lag, whole, oa_right)
        each(0, count, whole_head)

        def drain(count):
            sent(early_kv.at[:, 0:count], 0)
            sent(pack_s.at[count:whole], 1)
            sent(st_s.at[count:whole], 2)
            sent(oa_s.at[count:whole], 3)

        by_early(drain)
        sent(whole_out, 4)

    @pl.when(me == 2)
    def _():
        def start(h):
            move(
                q_ref.at[:, cols(h)], qq.at[0, :, cols(h)], sem_s.at[0], sem_b.at[h], 1
            ).start()

        def relay(h):
            start(h)
            q3 = qq.at[1, :, cols(h)]
            arrived(q3, sem_b.at[h])
            move(q3, q3, sem_s.at[5], sem_b.at[h], 1).start()

        each(early, early + DIRECT, start)
        each(early + DIRECT, whole, relay)
        for c in range(count):
            for i, src, sem in ((0, k_ref, c), (1, v_ref, c), (5, q_ref, count + c)):
                to_whole(c, i, src, sem)

        wait_loads()

        def pass_on(h, level, out):
            pack_s[h, :HEAD] = out.astype(jnp.bfloat16)
            st_s[h, 0:1] = level
            st_s[h, 1:2] = level
            pack_right(h, 2, 3)
            st_right(h, 3, 3)

        def early_head(h):
            q, k, v = own_qkv(h)
            arrived(early_kv.at[:, h], sem_a.at[h])
            arrived(qq.at[1, :, cols(h)], sem_b.at[h])
            k0, v0, k1, v1 = [early_kv[i, h] for i in range(4)]
            phi_k = feature_map(k)
            before = tn(feature_map(k0), v0) + tn(feature_map(k1), v1)
            put_state(h, before + tn(phi_k, v))
            q3 = qq[1, :, cols(h)]
            other = soft([nt(k0, q3), nt(k1, q3), nt(k, q3)], [v0, v1, v])
            pass_on(h, *normalised(other))
            phi_q, linear = local_linear(q, phi_k, v)
            linear = linear + tt(before.astype(jnp.bfloat16), phi_q)
            scores = [nt(k0, q), nt(k1, q), diagonal(q, k)]
            finish(h, soft(scores, [v0, v1, v]), linear)

        each(0, early, early_head)

        def for_last(h):
            k, v = own[1, :, cols(h)], own[2, :, cols(h)]
            state = tn(feature_map(k), v)

            @pl.when(h < early + DIRECT)
            def _():
                arrived(qq.at[1, :, cols(h)], sem_w.at[spare + h - early])

            other = soft([nt(k, qq[1, :, cols(h)])], [v])
            pack_arrived(h)
            put_state(h, get_state(h).astype(jnp.float32) + state)
            pass_on(h, *normalised(merge(other, st_r[h, 1:2], pack_r[h, :HEAD])))

        def for_own(h):
            q, k, v = own_qkv(h)
            phi_q, linear = local_linear(q, feature_map(k), v)
            linear = linear + tt(get_state(h), phi_q)
            own_sum = soft([diagonal(q, k)], [v])
            arrived(oa_r.at[h], sem_b.at[h])
            finish(h, merge(own_sum, st_r[h, 0:1], oa_r[h]), linear)

        def head(h):
            for_last(h)
            in_turn(h, for_own)

        each(early, whole, head)
        each(whole - lag, whole, for_own)


        def drain(count):
            sent(qq.at[0, :, count * HEAD : whole * HEAD], 0)
            sent(qq.at[1, :, (count + DIRECT) * HEAD : whole * HEAD], 5)

        by_early(drain)
        sent(whole_in.at[:, 0:3], 1)
        sent(pack_s.at[0:whole], 2)
        sent(st_s.at[0:whole], 3)
        arrived(out_ref.at[:, whole * HEAD :], sem_w.at[2 * count])

    @pl.when(me == 3)
    def _():
        def to_hub(h):
            move(
                q_ref.at[:, cols(h)], qq.at[1, :, cols(h)], sem_s.at[2], sem_b.at[h], 1
            ).start()

        def to_left(h, sem):
            move(q_ref.at[:, cols(h)], qq.at[1, :, cols(h)], sem_s.at[0], sem, 2).start()

        each(early, early + DIRECT, to_hub)
        each(early + DIRECT, whole, lambda h: to_left(h, sem_b.at[h]))
        each(0, early, lambda h: to_left(h, sem_b.at[h]))
        each(0, DIRECT, lambda i: to_left(early + i, sem_w.at[spare + i]))

        wait_loads()

        def compute(h):
            q, k, v = own_qkv(h)
            phi_q, linear = local_linear(q, feature_map(k), v)
            own_sum = soft([diagonal(q, k)], [v])
            pack_arrived(h)
            linear = linear + tt(get_state(h), phi_q)
            finish(h, merge(own_sum, st_r[h, 0:1], pack_r[h, :HEAD]), linear)

        each(0, turn, compute)
        for c in range(count):
            for i, src in enumerate((q_ref, k_ref, v_ref)):
                to_whole(c, 2 + i, src, c)
        each(turn, whole, compute)

        sent(qq.at[1, :, : whole * HEAD], 0)
        sent(whole_in.at[:, 0:3], 1)
        by_early(lambda count: sent(qq.at[1, :, count * HEAD : (count + DIRECT) * HEAD], 2))
        arrived(out_ref.at[:, whole * HEAD :], sem_w.at[2 * count])


def hub_shards(queries, key_vectors, value_vectors, norm_gain, window_gain):
    tok, width = queries.shape
    heads = width // HEAD
    most, _, _, whole = classes(heads)
    count = heads - whole
    hbm = pl.BlockSpec(memory_space=pl.ANY)
    pack = pltpu.VMEM((heads, HEAD + HEAD * HEAD // tok, tok), jnp.bfloat16)
    partial = pltpu.VMEM((heads, HEAD, tok), jnp.bfloat16)
    stats = pltpu.VMEM((heads, 2, tok), jnp.float32)
    dma = pltpu.SemaphoreType.DMA
    return pl.pallas_call(
        hub_kernel,
        out_shape=pltpu.VMEM((tok, width), jnp.bfloat16),
        in_specs=[hbm] * 5,
        out_specs=pl.BlockSpec(memory_space=pltpu.VMEM),
        scratch_shapes=[
            pltpu.VMEM((2, tok, width), jnp.bfloat16),
            pltpu.VMEM((2, tok, width), jnp.bfloat16),
            pltpu.VMEM((3, tok, width), jnp.bfloat16),
            pltpu.VMEM((2, heads, HEAD), jnp.float32),
            pltpu.VMEM((4, most, tok, HEAD), jnp.bfloat16),
            pltpu.VMEM((count, 6, tok, HEAD), jnp.bfloat16),
            pltpu.VMEM((count, 2, tok, HEAD), jnp.bfloat16),
        ]
        + [pack] * 2
        + [partial] * 2
        + [stats] * 2
        + [pltpu.VMEM(((HEAD + HEAD * HEAD // tok) // 4 + 1, 2, tok), jnp.float32)]
        + [dma((heads,))] * 2
        + [dma((2 * count + 1 + DIRECT,)), dma((6,)), dma((2,))],
        compiler_params=pltpu.CompilerParams(
            collective_id=0, has_side_effects=True, vmem_limit_bytes=56 * 2**20
        ),
        name="hub_attention",
    )(
        queries,
        key_vectors,
        value_vectors,
        norm_gain.reshape(heads, HEAD),
        window_gain.reshape(heads, HEAD),
    )


def solution(mesh):
    count = mesh.shape["ctx"]

    def run(queries, key_vectors, value_vectors, norm_gain, window_gain):
        args = (queries, key_vectors, value_vectors, norm_gain, window_gain)
        fits = count * queries.shape[0] <= WINDOW
        tok, width = queries.shape
        even = tok % HEAD == 0 and HEAD * HEAD % (16 * tok) == 0
        if fits and even and count == 4 and width >= 16 * HEAD:
            return hub_shards(*args)
        return shards(*args)

    return jax.shard_map(
        run,
        mesh=mesh,
        in_specs=(P(("dp", "ctx"), None), P(("dp", "ctx"), None), P(("dp", "ctx"), None), P(), P()),
        out_specs=P(("dp", "ctx"), None),
        check_vma=False,
    )
```
